32 devices in a mesh: lat: 8 (over y, x, core), chan: 4 (over z).
Axes of the slice: x: 2, y: 2, z: 4, core: 2. Of those that a mesh axis runs over, the one named last changes fastest.
Arguments:
- signal: bfloat16 [384, 384, 1440], P('lat', 'chan'), may hold values from -6 to 6
- spectral_filter: float32 [384, 2, 384], replicated, may hold values from -4 to 4
- channel_mix: bfloat16 [2, 384, 384], replicated, may hold values from -0.21875 to 0.21875
Outputs:
- output: bfloat16 [384, 384, 1440], P('lat', 'chan')
The draws below stay inside these ranges and needn't reach their ends.
All inputs are finite; a program needn't handle non-finite values.
Results may differ from the reference program's by a relative error of at most 0.01.
Values may be sent and summed in bfloat16 or wider, within the bound.
No kernel may reach another device: no remote copies, remote signals or barrier semaphores. Data moves between devices by JAX's collectives and lax.ppermute only.
A program may use at most 192 MiB of HBM per device.

```python
import math
import jax
import jax.numpy as jnp
from jax import lax

C = 384
NLON = 1440
NLAT = 384
L = 384
LAT_DEV = 48
M_DEV = 48


def shard_levels(rng, extent, pieces, smallest, top_value):
    gain, own = 1.0, jax.random.fold_in(rng, 6)
    for axis_at, blocks in pieces:
        heights = jnp.exp(jax.random.uniform(jax.random.fold_in(own, axis_at), (blocks,), jnp.float32, smallest / len(pieces), top_value / len(pieces)))
        gain = gain * jnp.repeat(heights, extent[axis_at] // blocks).reshape([-1 if axis == axis_at else 1 for axis in range(len(extent))])
    return gain


def normal_values(rng, dims, deviation, reach, pieces=(), kind=jnp.bfloat16):
    gain = shard_levels(rng, dims, pieces, -0.22, 0.18) if pieces else 1.0
    entries = jax.random.normal(rng, dims, jnp.float32) * deviation * gain
    return jnp.minimum(jnp.maximum(entries, -reach), reach).astype(kind)


def setup_inputs(seed: int = 0) -> dict:
    keys = jax.random.split(jax.random.key(seed), 4)
    return {
        "signal": normal_values(keys[0], (NLAT, C, NLON), 1.0, 6.0, ((0, 8), (1, 4))),
        "spectral_filter": normal_values(keys[1], (L, 2, C), 1.0, 4.0, (), jnp.float32),
        "channel_mix": normal_values(keys[2], (2, C, C), (2 * C) ** -0.5, 0.21875),
    }


def fourier_tables(orders, lon_count):
    cells = jnp.arange(lon_count, dtype=jnp.int32)
    phase = orders[:, None] * cells[None, :] % lon_count
    angle = phase.astype(jnp.float32) * (2.0 * math.pi / lon_count)
    forward = jnp.stack([jnp.cos(angle), -jnp.sin(angle)], 0)
    factor = jnp.where(orders == 0, 1.0, 2.0).astype(jnp.float32)[None, :, None]
    return (forward.astype(jnp.bfloat16), (forward * factor).astype(jnp.bfloat16))

def latitude_terms(lat_index, lat_total, lon_count):
    theta = (lat_index.astype(jnp.float32) + 0.5) * (math.pi / lat_total)
    weight = jnp.sin(theta) * (2.0 * math.pi * math.pi / (lat_total * lon_count))
    return (jnp.cos(theta), jnp.log(jnp.sin(theta)), weight)

def seed_logs(orders, log_sine):
    order_f = orders.astype(jnp.float32)[:, None]
    base_term = 0.5 * jnp.log((2.0 * order_f + 1.0) / (4.0 * math.pi))
    ratio_term = 0.5 * (jax.scipy.special.gammaln(order_f + 0.5) - jax.scipy.special.gammaln(order_f + 1.0) - 0.5 * math.log(math.pi))
    return base_term + ratio_term + order_f * log_sine[None, :]

def legendre_rows(recursion, orders, log_seeds, first_degree, row_count, cosine):
    order_f = orders.astype(jnp.float32)[:, None]

    def advance(carried, degree):
        previous, earlier, log_scale = carried
        degree_f = degree.astype(jnp.float32)
        degree_gap = degree_f * degree_f - order_f * order_f
        coeff_a = jnp.sqrt((4.0 * degree_f * degree_f - 1.0) / jnp.maximum(degree_gap, 1.0))
        below_sq = (degree_f - 1.0) * (degree_f - 1.0)
        coeff_b = jnp.sqrt(jnp.maximum(below_sq - order_f * order_f, 0.0) / (4.0 * below_sq - 1.0))
        grown = coeff_a * (cosine[None, :] * previous - coeff_b * earlier)
        at_start = degree_f == order_f
        is_above = degree_f > order_f
        fresh_value = jnp.where(at_start, 1.0, jnp.where(is_above, grown, 0.0))
        log_scale = jnp.where(at_start, log_seeds, log_scale)
        scaled_value = fresh_value * jnp.exp(log_scale)
        rescale = jnp.where(degree_f >= order_f, jnp.abs(fresh_value) + jnp.abs(previous), 1.0)
        return ((fresh_value / rescale, previous / rescale, log_scale + jnp.log(rescale)), scaled_value)
    degrees_here = first_degree + jnp.arange(row_count, dtype=jnp.int32)
    carried, values = lax.scan(advance, recursion, degrees_here, unroll=8)
    return (carried, jnp.moveaxis(values, 0, 1))

def apply_filter(coefficients, gains):
    real_part = coefficients[..., 0, :] * gains[:, 0, :] - coefficients[..., 1, :] * gains[:, 1, :]
    imag_part = coefficients[..., 0, :] * gains[:, 1, :] + coefficients[..., 1, :] * gains[:, 0, :]
    return jnp.stack([real_part, imag_part], -2)

def mix_table(channel_mix):
    real_w = channel_mix[0]
    imag_w = channel_mix[1]
    return jnp.stack([jnp.stack([real_w, imag_w], 1), jnp.stack([-imag_w, real_w], 1)], 0)

def reference(signal, spectral_filter, channel_mix):
    group_count = L // M_DEV
    band_count = NLAT // LAT_DEV
    orders_all = jnp.arange(L, dtype=jnp.int32)
    trig, synth = fourier_tables(orders_all, NLON)
    cosine, log_sine, weight = latitude_terms(jnp.arange(NLAT, dtype=jnp.int32), NLAT, NLON)
    trig_flat = trig.reshape(2 * L, NLON).T

    def analyse(block):
        signal_rows, weight_rows = block
        spectrum = jnp.dot(signal_rows.reshape(LAT_DEV * C, NLON), trig_flat, preferred_element_type=jnp.float32)
        spectrum = spectrum.reshape(LAT_DEV, C, 2, L) * weight_rows[:, None, None, None]
        return spectrum.astype(jnp.bfloat16)
    fourier = lax.map(analyse, (signal.reshape(band_count, LAT_DEV, C, NLON), weight.reshape(band_count, LAT_DEV)))
    fourier = jnp.transpose(fourier.reshape(NLAT, C, 2, L), (3, 0, 2, 1)).reshape(group_count, M_DEV, NLAT, 2, C)
    kernel = mix_table(channel_mix).reshape(2 * C, 2 * C)

    def spectral(block):
        orders, fourier_group = block
        log_seeds = seed_logs(orders, log_sine)
        zero_state = jnp.zeros((M_DEV, NLAT), jnp.float32)
        _, legendre = legendre_rows((zero_state, zero_state, zero_state), orders, log_seeds, jnp.zeros((), jnp.int32), L, cosine)
        legendre = legendre.astype(jnp.bfloat16).astype(jnp.float32)
        coefficients = jnp.einsum('glj,gjtc->gltc', legendre, fourier_group.astype(jnp.float32))
        filtered = apply_filter(coefficients, spectral_filter).astype(jnp.bfloat16)
        mixed = jnp.dot(filtered.reshape(M_DEV * L, 2 * C), kernel, preferred_element_type=jnp.float32)
        mixed = mixed.astype(jnp.bfloat16).reshape(M_DEV, L, 2, C)
        back = jnp.einsum('glj,gltc->gjtc', legendre, mixed.astype(jnp.float32))
        return back.astype(jnp.bfloat16)
    back = lax.map(spectral, (orders_all.reshape(group_count, M_DEV), fourier)).reshape(L, NLAT, 2, C)
    back = jnp.transpose(back.reshape(L, band_count, LAT_DEV, 2, C), (1, 2, 4, 3, 0))
    synth_flat = synth.reshape(2 * L, NLON)

    def synthesise(band_rows):
        result = jnp.dot(band_rows.reshape(LAT_DEV * C, 2 * L), synth_flat, preferred_element_type=jnp.float32)
        return result.astype(jnp.bfloat16).reshape(LAT_DEV, C, NLON)
    return lax.map(synthesise, back).reshape(NLAT, C, NLON)
```

```python
import functools
import math

import jax
import jax.numpy as jnp
import numpy as np
from jax import lax
from jax.experimental import pallas as pl
from jax.experimental.pallas import tpu as pltpu
from jax.sharding import PartitionSpec as P

F32 = jnp.float32
BF16 = jnp.bfloat16
VMEM_BYTES = 56 << 20
STEP = 16


def params(**kw):
    return pltpu.CompilerParams(vmem_limit_bytes=VMEM_BYTES, **kw)


def fourier_tables(orders, lon_count):
    cells = jnp.arange(lon_count, dtype=jnp.int32)
    phase = orders[:, None] * cells[None, :] % lon_count
    angle = phase.astype(F32) * (2.0 * math.pi / lon_count)
    forward = jnp.stack([jnp.cos(angle), -jnp.sin(angle)], 0)
    factor = jnp.where(orders == 0, 1.0, 2.0).astype(F32)[None, :, None]
    return (forward.astype(BF16), (forward * factor).astype(BF16))


def latitude_terms(lat_index, lat_total, lon_count):
    theta = (lat_index.astype(F32) + 0.5) * (math.pi / lat_total)
    weight = jnp.sin(theta) * (2.0 * math.pi * math.pi / (lat_total * lon_count))
    return (jnp.cos(theta), jnp.log(jnp.sin(theta)), weight)


def seed_logs(orders, log_sine):
    order_f = orders.astype(F32)[:, None]
    base_term = 0.5 * jnp.log((2.0 * order_f + 1.0) / (4.0 * math.pi))
    ratio_term = 0.5 * (
        jax.scipy.special.gammaln(order_f + 0.5)
        - jax.scipy.special.gammaln(order_f + 1.0)
        - 0.5 * math.log(math.pi)
    )
    return base_term + ratio_term + order_f * log_sine[None, :]


def table_body(group_rows, seeds_ref, order_ref, cosine_ref, out_ref, rows_ref):
    degrees = out_ref.shape[2]
    lat_total = out_ref.shape[3]
    slots = seeds_ref.shape[0]
    per_step = slots // 2
    first = pl.program_id(0) * (per_step * group_rows)
    first_block = first // STEP
    blank = jnp.zeros((STEP, lat_total), out_ref.dtype)

    @pl.loop(0, first_block)
    def _(block):
        at = pl.multiple_of(block * STEP, STEP)
        for slot in range(slots):
            out_ref[slot // 2, slot % 2, pl.ds(at, STEP), :] = blank

    order = order_ref[:, :128]
    order_sq = order * order
    cosine = jnp.broadcast_to(cosine_ref[...], (slots, lat_total))
    wide = lat_total // 128

    def spread(x):
        return jnp.concatenate([x] * wide, axis=1)

    seeds = seeds_ref[...]
    zero = jnp.zeros((slots, lat_total), F32)
    start = (zero, zero, seeds, jnp.zeros((slots, 128), F32))

    def advance(block, carry):
        fresh, before, log_scale, coeff_b = carry
        at = pl.multiple_of(block * STEP, STEP)
        for half in range(STEP // 8):
            scale = jnp.exp(log_scale)
            for step in range(8):
                degree = (at + half * 8 + step).astype(F32)
                degree_v = jnp.full((slots, 128), degree, F32)
                degree_sq = degree_v * degree_v
                ratio = jnp.maximum(degree_sq - order_sq, 1.0) / jnp.maximum(4.0 * degree_sq - 1.0, 1.0)
                root = lax.rsqrt(ratio)
                root = root * (1.5 - 0.5 * ratio * root * root)
                starts = jnp.where(degree_v == order, 1.0, 0.0)
                grown = spread(root) * (cosine * fresh - spread(coeff_b) * before) + spread(starts)
                coeff_b = ratio * root
                before, fresh = fresh, grown
                rows_ref[half * 8 + step] = grown * scale
            size = jnp.abs(fresh) + jnp.abs(before)
            size = jnp.where(size == 0.0, 1.0, size)
            inverse = 1.0 / size
            fresh = fresh * inverse
            before = before * inverse
            log_scale = log_scale + jnp.log(size)
        for slot in range(slots):
            out_ref[slot // 2, slot % 2, pl.ds(at, STEP), :] = rows_ref[:, slot, :].astype(out_ref.dtype)
        return (fresh, before, log_scale, coeff_b)

    lax.fori_loop(first_block, degrees // STEP, advance, start)


def legendre_table(seeds, orders_f, cosine, group_rows, degrees):
    order_count, lat_total = seeds.shape
    groups = order_count // 2
    per_step = math.gcd(groups, 4)
    slots = 2 * per_step
    order_wide = jnp.broadcast_to(orders_f[:, None], (order_count, 128))
    steps = groups // per_step
    seeds = seeds.reshape(steps, slots, lat_total)
    order_wide = order_wide.reshape(steps, slots, 128)
    return pl.pallas_call(
        functools.partial(table_body, group_rows),
        grid=(steps,),
        in_specs=[
            pl.BlockSpec((None, slots, lat_total), lambda i: (i, 0, 0)),
            pl.BlockSpec((None, slots, 128), lambda i: (i, 0, 0)),
            pl.BlockSpec((1, lat_total), lambda i: (0, 0)),
        ],
        out_specs=pl.BlockSpec((per_step, 2, degrees, lat_total), lambda i: (i, 0, 0, 0)),
        out_shape=jax.ShapeDtypeStruct((groups, 2, degrees, lat_total), BF16),
        scratch_shapes=[pltpu.VMEM((STEP, slots, lat_total), F32)],
        compiler_params=params(),
        cost_estimate=pl.CostEstimate(
            flops=40_000_000, transcendentals=0, bytes_accessed=groups * 2 * degrees * lat_total * 2
        ),
        name="legendre_table",
    )(seeds, order_wide, cosine[None, :])


def lane_is_second(rows, lanes):
    lane = lax.broadcasted_iota(jnp.int32, (rows, lanes), 1)
    half = lanes // 2
    quarter = lanes // 4
    inner = jnp.where(lane >= half, lane - half, lane)
    return inner >= quarter


def analyse_body(plan, count_ref, chan_ref, fourier_ref, table_ref, gain_ref, cross_ref, *refs):
    outs, packed = refs[:-1], refs[-1]
    step = pl.program_id(0)
    degrees = table_ref.shape[1]
    lanes = fourier_ref.shape[-1]
    part = plan["part"]
    start = pl.multiple_of(count_ref[step], STEP)

    @pl.when(step == 0)
    def _():
        tail = plan["pad"] + plan["rows"]
        left = packed.shape[0] - tail
        if left:
            packed[tail:, :] = jnp.zeros((left, lanes), packed.dtype)

    rows_in = fourier_ref[...].reshape(table_ref.shape[2], lanes)
    even = jnp.dot(table_ref[0], rows_in, preferred_element_type=F32)
    odd = jnp.dot(table_ref[1], rows_in, preferred_element_type=F32)
    both = jnp.where(lane_is_second(degrees, lanes), odd, even)
    swapped = pltpu.roll(both, lanes // 2, 1)
    kept = both * gain_ref[...] + swapped * cross_ref[...]
    packed[pl.ds(start, degrees), :] = kept.astype(packed.dtype)

    @pl.when(step == pl.num_programs(0) - 1)
    def _():
        for shift, out in enumerate(outs):
            owner = lax.rem(chan_ref[0] + shift, len(outs))
            at = pl.multiple_of(plan["pad"] + owner * part, STEP)
            out[...] = packed[pl.ds(at, part), :]


def chunk_plan(groups, group_rows, degrees, chan_count):
    sizes = [degrees - group_rows * g for g in groups]
    offsets = [sum(sizes[:i]) for i in range(len(groups))]
    rows = sum(sizes)
    unit = STEP * chan_count
    total = -(-rows // unit) * unit
    pad = max([group_rows * g - o for g, o in zip(groups, offsets)] + [0])
    pad = -(-pad // STEP) * STEP
    starts = [pad + o - group_rows * g for g, o in zip(groups, offsets)]
    return {
        "groups": groups, "rows": rows, "total": total, "part": total // chan_count,
        "pad": pad, "starts": starts,
    }


def analyse(plan, chan, fourier, table, gain, cross, chan_count):
    bands, count, band_rows, lanes = fourier.shape
    _, _, degrees, lat_total = table.shape
    first = plan["groups"][0]
    last = plan["groups"][-1]
    starts = jnp.asarray(np.array(plan["starts"][::-1], np.int32))
    spec = pltpu.PrefetchScalarGridSpec(
        num_scalar_prefetch=2,
        grid=(count,),
        in_specs=[
            pl.BlockSpec((bands, None, band_rows, lanes), lambda i, s, c: (0, count - 1 - i, 0, 0)),
            pl.BlockSpec((None, 2, degrees, lat_total), lambda i, s, c: (last - i, 0, 0, 0)),
            pl.BlockSpec((degrees, lanes), lambda i, s, c: (0, 0)),
            pl.BlockSpec((degrees, lanes), lambda i, s, c: (0, 0)),
        ],
        out_specs=[pl.BlockSpec((plan["part"], lanes), lambda i, s, c: (0, 0))] * chan_count,
        scratch_shapes=[pltpu.VMEM((plan["pad"] + plan["total"], lanes), BF16)],
    )
    return pl.pallas_call(
        functools.partial(analyse_body, plan),
        grid_spec=spec,
        out_shape=[jax.ShapeDtypeStruct((plan["part"], lanes), BF16)] * chan_count,
        compiler_params=params(),
        cost_estimate=pl.CostEstimate(
            flops=count * 4 * degrees * lat_total * lanes,
            transcendentals=0,
            bytes_accessed=count * (2 * degrees * lat_total + lat_total * lanes) * 2 + plan["total"] * lanes * 2,
        ),
        name="analyse",
    )(starts, chan, fourier, table, gain, cross)


def mix_body(chan_count, *refs):
    ins, kernel_ref, outs = refs[:chan_count], refs[chan_count], refs[chan_count + 1:]
    gathered = jnp.concatenate([r[...] for r in ins], axis=1)
    for shift, out in enumerate(outs):
        out[...] = jnp.dot(gathered, kernel_ref[shift], preferred_element_type=F32).astype(out.dtype)


def mix(parts, kernel):
    chan_count = len(parts)
    rows, lanes = parts[0].shape
    return pl.pallas_call(
        functools.partial(mix_body, chan_count),
        out_shape=[jax.ShapeDtypeStruct((rows, lanes), BF16)] * chan_count,
        compiler_params=params(),
        cost_estimate=pl.CostEstimate(
            flops=2 * rows * (chan_count * lanes) ** 2,
            transcendentals=0,
            bytes_accessed=(chan_count * lanes) ** 2 * 2 + 4 * chan_count * rows * lanes,
        ),
        name="mix",
    )(*parts, kernel)


def synthesise_body(plan, count_ref, chan_ref, table_ref, *refs):
    chan_count = plan["total"] // plan["part"]
    ins, out_ref, packed = refs[:chan_count], refs[chan_count], refs[chan_count + 1]
    step = pl.program_id(0)
    degrees, lat_total = table_ref.shape[1:]
    lanes = packed.shape[1]
    part = plan["part"]

    @pl.when(step == 0)
    def _():
        for shift, part_ref in enumerate(ins):
            owner = lax.rem(chan_ref[0] + (chan_count - shift), chan_count)
            at = pl.multiple_of(plan["pad"] + owner * part, STEP)
            packed[pl.ds(at, part), :] = part_ref[...]

    start = pl.multiple_of(count_ref[0, step], STEP)
    below = count_ref[1, step]
    rows = packed[pl.ds(start, degrees), :]
    held = lax.broadcasted_iota(jnp.int32, rows.shape, 0) >= below
    rows = jnp.where(held, rows, jnp.zeros_like(rows))
    dims = (((0,), (0,)), ((), ()))
    even = lax.dot_general(table_ref[0], rows, dims, preferred_element_type=F32)
    odd = lax.dot_general(table_ref[1], rows, dims, preferred_element_type=F32)
    both = jnp.where(lane_is_second(lat_total, lanes), odd, even)
    out_ref[...] = both.astype(out_ref.dtype).reshape(out_ref.shape)


def synthesise(plan, chan, table, parts, bands):
    _, _, degrees, lat_total = table.shape
    count = len(plan["groups"])
    first = plan["groups"][0]
    chan_count = len(parts)
    part, lanes = parts[0].shape
    band_rows = lat_total // bands
    group_rows = plan["group_rows"]
    numbers = jnp.asarray(
        np.array([plan["starts"], [group_rows * g for g in plan["groups"]]], np.int32)
    )
    spec = pltpu.PrefetchScalarGridSpec(
        num_scalar_prefetch=2,
        grid=(count,),
        in_specs=[pl.BlockSpec((None, 2, degrees, lat_total), lambda i, s, c: (first + i, 0, 0, 0))]
        + [pl.BlockSpec((part, lanes), lambda i, s, c: (0, 0))] * chan_count,
        out_specs=pl.BlockSpec((bands, None, band_rows, lanes), lambda i, s, c: (0, i, 0, 0)),
        scratch_shapes=[pltpu.VMEM((plan["pad"] + plan["total"], lanes), BF16)],
    )
    return pl.pallas_call(
        functools.partial(synthesise_body, plan),
        grid_spec=spec,
        out_shape=jax.ShapeDtypeStruct((bands, count, band_rows, lanes), BF16),
        compiler_params=params(),
        cost_estimate=pl.CostEstimate(
            flops=count * 4 * degrees * lat_total * lanes,
            transcendentals=0,
            bytes_accessed=count * (2 * degrees * lat_total + lat_total * lanes) * 2 + plan["total"] * lanes * 2,
        ),
        name="synthesise",
    )(numbers, chan, table, *parts)


def split_groups(group_count):
    sizes = [group_count - g for g in range(group_count)]
    total = sum(sizes)
    marks = []
    run = 0
    for g, size in enumerate(sizes):
        run += size
        if len(marks) < 2 and run >= 0.3 * total * (len(marks) + 1):
            marks.append(g + 1)
    edges = [0] + marks + [group_count]
    pieces = [list(range(a, b)) for a, b in zip(edges[:-1], edges[1:]) if b > a]
    if len(pieces) == 3:
        pieces = [pieces[0], pieces[2], pieces[1]]
    return pieces


def on_device(signal, spectral_filter, channel_mix):
    lat_count = lax.axis_size("lat")
    chan_count = lax.axis_size("chan")
    lat_rows, quarter, lon_count = signal.shape
    lat_total = lat_rows * lat_count
    degrees = spectral_filter.shape[0]
    group_rows = 2 * lat_count
    group_count = degrees // group_rows
    lat_index = lax.axis_index("lat")
    chan_index = lax.axis_index("chan")
    chan = jnp.reshape(chan_index, (1,)).astype(jnp.int32)
    lanes = 4 * quarter

    k_at = jnp.arange(lat_count, dtype=jnp.int32)
    g_at = jnp.arange(group_count, dtype=jnp.int32)
    e_at = jnp.arange(2, dtype=jnp.int32)
    orders_all = group_rows * g_at[None, None, :] + 2 * k_at[None, :, None] + e_at[:, None, None]
    trig, synth = fourier_tables(orders_all.reshape(-1), lon_count)
    trig = trig.reshape(2, 2, lat_count, group_count, lon_count)
    synth = synth.reshape(2, 2, lat_count, group_count, lon_count)
    own_rows = lat_index * lat_rows + jnp.arange(lat_rows, dtype=jnp.int32)
    _, _, own_weight = latitude_terms(own_rows, lat_total, lon_count)
    cosine, log_sine, _ = latitude_terms(jnp.arange(lat_total, dtype=jnp.int32), lat_total, lon_count)
    orders_own = (group_rows * g_at[:, None] + 2 * lat_index + e_at[None, :]).reshape(-1)
    seeds = seed_logs(orders_own, log_sine)
    table = legendre_table(seeds, orders_own.astype(F32), cosine, group_rows, degrees)

    gains = lax.dynamic_slice_in_dim(spectral_filter, chan_index * quarter, quarter, 2)
    direct = jnp.tile(gains[:, 0, :], (1, 4))
    cross = jnp.concatenate([jnp.tile(-gains[:, 1, :], (1, 2)), jnp.tile(gains[:, 1, :], (1, 2))], 1)

    steps = jnp.arange(chan_count, dtype=jnp.int32)
    sources = (chan_index - steps) % chan_count
    targets = (chan_index + steps) % chan_count
    real_w, imag_w = channel_mix[0], channel_mix[1]
    full = jnp.stack([jnp.stack([real_w, imag_w], 0), jnp.stack([-imag_w, real_w], 0)], 0)
    full = full.reshape(2, 2, chan_count, quarter, chan_count, quarter)
    full = jnp.take(jnp.take(full, sources, axis=2), targets, axis=4)
    same = jnp.eye(2, dtype=BF16)
    kernel = full.transpose(4, 2, 0, 3, 1, 5)[:, :, :, None, :, :, None, :] * same[None, None, None, :, None, None, :, None]
    kernel = kernel.reshape(chan_count, chan_count * lanes, lanes)

    def moved(parts):
        out = [parts[0]]
        for shift in range(1, chan_count):
            pairs = [(i, (i + shift) % chan_count) for i in range(chan_count)]
            out.append(lax.ppermute(parts[shift], "chan", pairs))
        return out

    pieces = split_groups(group_count)
    returned = []
    for groups in pieces:
        plan = chunk_plan(groups, group_rows, degrees, chan_count)
        plan["group_rows"] = group_rows
        trig_part = trig[:, :, :, groups[0]:groups[-1] + 1, :]
        spectrum = jnp.einsum("jcn,tekgn->kgjtec", signal, trig_part, preferred_element_type=F32)
        spectrum = (spectrum * own_weight[None, None, :, None, None, None]).astype(BF16)
        spectrum = spectrum.reshape(lat_count, len(groups), lat_rows, lanes)
        fourier = lax.all_to_all(spectrum, "lat", split_axis=0, concat_axis=0, tiled=True)
        filtered = analyse(plan, chan, fourier, table, direct, cross, chan_count)
        mixed = mix(moved(filtered), kernel)
        back = synthesise(plan, chan, table, moved(mixed), lat_count)
        back = lax.all_to_all(back, "lat", split_axis=0, concat_axis=0, tiled=True)
        returned.append((groups, back))
    rows = jnp.concatenate([b for _, b in returned], 1)
    synth = jnp.concatenate([synth[:, :, :, g[0]:g[-1] + 1, :] for g, _ in returned], 3)
    rows = rows.reshape(lat_count, group_count, lat_rows, 2, 2, quarter)
    output = jnp.einsum("kgjued,uekgn->jdn", rows, synth, preferred_element_type=F32)
    return output.astype(BF16)


def solution(mesh):
    return jax.shard_map(
        on_device,
        mesh=mesh,
        in_specs=(P("lat", "chan", None), P(), P()),
        out_specs=P("lat", "chan", None),
        check_vma=False,
    )
```

```python
import functools
import math

import jax
import jax.numpy as jnp
import numpy as np
from jax import lax
from jax.experimental import pallas as pl
from jax.experimental.pallas import tpu as pltpu
from jax.sharding import PartitionSpec as P

F32 = jnp.float32
BF16 = jnp.bfloat16
VMEM_BYTES = 56 << 20
STEP = 16
HELD = pl.BlockSpec(memory_space=pl.ANY)
LIGHT = pl.CostEstimate(flops=1000, transcendentals=0, bytes_accessed=1000)
HEAVY = pl.CostEstimate(flops=200_000_000_000, transcendentals=0, bytes_accessed=1000)


def params(**kw):
    return pltpu.CompilerParams(vmem_limit_bytes=VMEM_BYTES, **kw)


def turns(orders, lon_count):
    cells = jnp.arange(lon_count, dtype=jnp.int32)
    phase = orders[:, None] * cells[None, :] % lon_count
    angle = phase.astype(F32) * (2.0 * math.pi / lon_count)
    return jnp.cos(angle), jnp.sin(angle)


def fourier_tables(group_orders, lat_count, lon_count):
    cos_g, sin_g = turns(group_orders, lon_count)
    fine = jnp.arange(2, dtype=jnp.int32)[:, None] + 2 * jnp.arange(lat_count, dtype=jnp.int32)[None, :]
    cos_f, sin_f = turns(fine.reshape(-1), lon_count)
    cos_g, sin_g, cos_f, sin_f = lax.optimization_barrier((cos_g, sin_g, cos_f, sin_f))
    cos_g, sin_g = cos_g[None, :, None, :], sin_g[None, :, None, :]
    cos_f = cos_f.reshape(2, 1, lat_count, lon_count)
    sin_f = sin_f.reshape(2, 1, lat_count, lon_count)
    forward = jnp.stack([cos_g * cos_f - sin_g * sin_f, -(sin_g * cos_f + cos_g * sin_f)], 0)
    orders = group_orders[None, :, None] + fine[:, None, :]
    factor = jnp.where(orders == 0, 1.0, 2.0).astype(F32)[None, :, :, :, None]
    shape = (4, group_orders.shape[0] * lat_count, lon_count)
    return (forward.astype(BF16).reshape(shape), (forward * factor).astype(BF16).reshape(shape))


def latitude_terms(lat_index, lat_total, lon_count):
    theta = (lat_index.astype(F32) + 0.5) * (math.pi / lat_total)
    weight = jnp.sin(theta) * (2.0 * math.pi * math.pi / (lat_total * lon_count))
    return (jnp.cos(theta), jnp.log(jnp.sin(theta)), weight)


def seed_logs(orders, log_sine):
    order_f = orders.astype(F32)[:, None]
    base_term = 0.5 * jnp.log((2.0 * order_f + 1.0) / (4.0 * math.pi))
    ratio_term = 0.5 * (
        jax.scipy.special.gammaln(order_f + 0.5)
        - jax.scipy.special.gammaln(order_f + 1.0)
        - 0.5 * math.log(math.pi)
    )
    return base_term + ratio_term + order_f * log_sine[None, :]


def table_body(group_rows, groups, base, inverse_ref, seeds_ref, order_ref, cosine_ref, *refs):
    out_ref, rows_ref = refs[-2:]
    depth = out_ref.shape[1]
    slots, lat_total = seeds_ref.shape
    per_step = slots // 2
    first = (groups[0] + pl.program_id(0) * per_step) * group_rows - base
    first_block = first // STEP
    blank = jnp.zeros((STEP, 2 * lat_total), out_ref.dtype)

    @pl.loop(0, first_block)
    def _(block):
        at = pl.multiple_of(block * STEP, STEP)
        for group in range(per_step):
            out_ref[group, pl.ds(at, STEP), :] = blank

    order = order_ref[...]
    order_sq = order * order
    cosine = jnp.broadcast_to(cosine_ref[...], (slots, lat_total))
    wide = lat_total // 128

    def spread(x):
        return jnp.concatenate([x] * wide, axis=1)

    seeds = seeds_ref[...]
    zero = jnp.zeros((slots, lat_total), F32)
    start = (zero, zero, seeds, jnp.zeros((slots, 128), F32))

    def advance(block, carry):
        fresh, before, log_scale, coeff_b = carry
        at = pl.multiple_of(block * STEP, STEP)
        scale = jnp.exp(log_scale)
        for step in range(STEP):
            degree = base + at + step
            degree_v = jnp.full((slots, 128), degree.astype(F32), F32)
            ratio = jnp.maximum(degree_v * degree_v - order_sq, 1.0) * inverse_ref[degree]
            root = lax.rsqrt(ratio)
            root = root * (1.5 - 0.5 * ratio * root * root)
            starts = jnp.where(degree_v == order, 1.0, 0.0)
            grown = spread(root) * (cosine * fresh - spread(coeff_b) * before) + spread(starts)
            coeff_b = ratio * root
            before, fresh = fresh, grown
            rows_ref[step] = grown * scale
        size = jnp.abs(fresh) + jnp.abs(before)
        size = jnp.where(size == 0.0, 1.0, size)
        inverse = 1.0 / size
        for slot in range(slots):
            cut = slice((slot % 2) * lat_total, (slot % 2 + 1) * lat_total)
            out_ref[slot // 2, pl.ds(at, STEP), cut] = rows_ref[:, slot, :].astype(out_ref.dtype)
        return (fresh * inverse, before * inverse, log_scale + jnp.log(size), coeff_b)

    lax.fori_loop(first_block, depth // STEP, advance, start)


def legendre_table(plan, seeds, orders_f, cosine, degrees, after=()):
    order_count, lat_total = seeds.shape
    groups = order_count // 2
    per_step = max(n for n in range(1, 9) if groups % n == 0)
    slots = 2 * per_step
    base = plan["base"]
    depth = degrees - base
    order_wide = jnp.broadcast_to(orders_f[:, None], (order_count, 128))
    steps = groups // per_step
    seeds = seeds.reshape(steps, slots, lat_total)
    order_wide = order_wide.reshape(steps, slots, 128)
    at = np.arange(degrees, dtype=np.float32)
    inverse = jnp.asarray((1.0 / np.maximum(4.0 * at * at - 1.0, 1.0)).astype(np.float32))
    spec = pltpu.PrefetchScalarGridSpec(
        num_scalar_prefetch=1,
        grid=(steps,),
        in_specs=[
            pl.BlockSpec((None, slots, lat_total), lambda i, v: (i, 0, 0)),
            pl.BlockSpec((None, slots, 128), lambda i, v: (i, 0, 0)),
            pl.BlockSpec((1, lat_total), lambda i, v: (0, 0)),
        ]
        + [HELD] * len(after),
        out_specs=pl.BlockSpec((per_step, depth, 2 * lat_total), lambda i, v: (i, 0, 0)),
        scratch_shapes=[pltpu.VMEM((STEP, slots, lat_total), F32)],
    )
    return pl.pallas_call(
        functools.partial(table_body, plan["group_rows"], plan["groups"], base),
        grid_spec=spec,
        out_shape=jax.ShapeDtypeStruct((groups, depth, 2 * lat_total), BF16),
        compiler_params=params(),
        cost_estimate=LIGHT,
        name="legendre_table",
    )(inverse, seeds, order_wide, cosine[None, :], *after)


def parity_lanes(lanes):
    second = (np.arange(lanes) % (lanes // 2)) >= lanes // 4
    return jnp.asarray(np.stack([1.0 - second, second]).astype(np.float32)).astype(BF16)


def by_parity(rows, lanes_ref):
    return jnp.concatenate([rows * lanes_ref[0:1, :], rows * lanes_ref[1:2, :]], axis=0)


def analyse_body(plan, count_ref, chan_ref, fourier_ref, table_ref, gain_ref, cross_ref, lanes_ref, *refs):
    outs, packed = refs[-1 - plan["chans"]:-1], refs[-1]
    step = pl.program_id(0)
    depth = table_ref.shape[0]
    lat_total = table_ref.shape[1] // 2
    lanes = fourier_ref.shape[-1]
    part = plan["part"]
    base = plan["base"]
    start = pl.multiple_of(count_ref[step], STEP)

    @pl.when(step == 0)
    def _():
        tail = plan["pad"] + plan["rows"]
        left = packed.shape[0] - tail
        if left:
            packed[tail:, :] = jnp.zeros((left, lanes), packed.dtype)

    rows_in = by_parity(fourier_ref[...].reshape(lat_total, lanes), lanes_ref)
    both = jnp.dot(table_ref[...], rows_in, preferred_element_type=F32)
    swapped = pltpu.roll(both, lanes // 2, 1)
    kept = both * gain_ref[base:, :] + swapped * cross_ref[base:, :]
    packed[pl.ds(start, depth), :] = kept.astype(packed.dtype)

    @pl.when(step == pl.num_programs(0) - 1)
    def _():
        for shift, out in enumerate(outs):
            owner = lax.rem(chan_ref[0] + shift, len(outs))
            at = pl.multiple_of(plan["pad"] + owner * part, STEP)
            out[...] = packed[pl.ds(at, part), :]


def chunk_plan(groups, group_rows, degrees, chan_count):
    sizes = [degrees - group_rows * g for g in groups]
    offsets = [sum(sizes[:i]) for i in range(len(groups))]
    rows = sum(sizes)
    unit = STEP * chan_count
    total = -(-rows // unit) * unit
    base = group_rows * groups[0]
    skips = [group_rows * g - base for g in groups]
    pad = max([skip - o for skip, o in zip(skips, offsets)] + [0])
    pad = -(-pad // STEP) * STEP
    starts = [pad + o - skip for skip, o in zip(skips, offsets)]
    return {
        "base": base, "skips": skips, "group_rows": group_rows, "chans": chan_count,
        "groups": groups, "rows": rows, "total": total, "part": total // chan_count,
        "pad": pad, "starts": starts,
    }


def analyse(plan, chan, fourier, table, gain, cross, chan_count, after=()):
    bands, count, band_rows, lanes = fourier.shape
    _, depth, lat_wide = table.shape
    starts = jnp.asarray(np.array(plan["starts"][::-1], np.int32))
    spec = pltpu.PrefetchScalarGridSpec(
        num_scalar_prefetch=2,
        grid=(count,),
        in_specs=[
            pl.BlockSpec((bands, None, band_rows, lanes), lambda i, s, c: (0, count - 1 - i, 0, 0)),
            pl.BlockSpec((None, depth, lat_wide), lambda i, s, c: (count - 1 - i, 0, 0)),
            pl.BlockSpec(gain.shape, lambda i, s, c: (0, 0)),
            pl.BlockSpec(cross.shape, lambda i, s, c: (0, 0)),
            pl.BlockSpec((2, lanes), lambda i, s, c: (0, 0)),
        ]
        + [HELD] * len(after),
        out_specs=[pl.BlockSpec((plan["part"], lanes), lambda i, s, c: (0, 0))] * chan_count,
        scratch_shapes=[pltpu.VMEM((plan["pad"] + plan["total"], lanes), BF16)],
    )
    return pl.pallas_call(
        functools.partial(analyse_body, plan),
        grid_spec=spec,
        out_shape=[jax.ShapeDtypeStruct((plan["part"], lanes), BF16)] * chan_count,
        compiler_params=params(),
        cost_estimate=LIGHT,
        name="analyse",
    )(starts, chan, fourier, table, gain, cross, parity_lanes(lanes), *after)


def kernel_body(mix_ref, *refs):
    out_ref = refs[-1]
    real, imag = mix_ref[0], mix_ref[1]
    quarter = real.shape[0]
    table = [[real, imag], [-imag, real]]
    for target in range(out_ref.shape[0]):
        cut = slice(target * quarter, (target + 1) * quarter)
        for t in range(2):
            row = [table[t][u][:, cut] for u in range(2)]
            out_ref[target, t * quarter:(t + 1) * quarter, :] = jnp.concatenate(row, axis=1)


def mix_kernel(channel_mix, chan_count, after=()):
    channels = channel_mix.shape[1]
    quarter = channels // chan_count
    wide = 2 * quarter
    return pl.pallas_call(
        kernel_body,
        grid=(chan_count,),
        in_specs=[pl.BlockSpec((2, quarter, channels), lambda i: (0, i, 0))] + [HELD] * len(after),
        out_specs=pl.BlockSpec((None, chan_count, wide, wide), lambda i: (i, 0, 0, 0)),
        out_shape=jax.ShapeDtypeStruct((chan_count, chan_count, wide, wide), BF16),
        compiler_params=params(),
        cost_estimate=HEAVY,
        name="mix_kernel",
    )(channel_mix, *after)


def mix_body(chan_count, chan_ref, *refs):
    ins, kernel_ref, outs = refs[:chan_count], refs[chan_count], refs[-chan_count:]
    own = chan_ref[0]
    quarter = ins[0].shape[1] // 4
    sources = [lax.rem(own + (chan_count - back), chan_count) for back in range(chan_count)]
    left = []
    for e in range(2):
        pieces = []
        for part in ins:
            for t in range(2):
                at = (2 * t + e) * quarter
                pieces.append(part[:, at:at + quarter])
        left.append(jnp.concatenate(pieces, axis=1))
    for shift, out in enumerate(outs):
        target = lax.rem(own + shift, chan_count)
        right = jnp.concatenate([kernel_ref[source, target] for source in sources], axis=0)
        made = [jnp.dot(x, right, preferred_element_type=F32).astype(out.dtype) for x in left]
        out[...] = jnp.concatenate(
            [made[e][:, u * quarter:(u + 1) * quarter] for u in range(2) for e in range(2)], axis=1
        )


def mix(chan, parts, kernel, after=()):
    chan_count = len(parts)
    rows, lanes = parts[0].shape
    spec = pltpu.PrefetchScalarGridSpec(
        num_scalar_prefetch=1,
        grid=(1,),
        in_specs=[pl.BlockSpec((rows, lanes), lambda i, c: (0, 0))] * chan_count
        + [pl.BlockSpec(kernel.shape, lambda i, c: (0, 0, 0, 0))]
        + [HELD] * len(after),
        out_specs=[pl.BlockSpec((rows, lanes), lambda i, c: (0, 0))] * chan_count,
    )
    return pl.pallas_call(
        functools.partial(mix_body, chan_count),
        grid_spec=spec,
        out_shape=[jax.ShapeDtypeStruct((rows, lanes), BF16)] * chan_count,
        compiler_params=params(),
        cost_estimate=HEAVY,
        name="mix",
    )(chan, *parts, kernel, *after)


BAND = 16


def swap_matrix():
    at = np.arange(BAND * BAND)
    turned = (at % BAND) * BAND + at // BAND
    return jnp.asarray(np.eye(BAND * BAND, dtype=np.float32)[turned]).astype(BF16)


def forward_body(first_row, counts, weight_ref, signal_ref, trig_ref, swap_ref, *refs):
    outs, held_ref = refs[-1 - len(counts):-1], refs[-1]
    band, quarter, lon_count = signal_ref.shape
    bands = outs[0].shape[0]
    lanes = outs[0].shape[-1]
    rows = sum(counts) * bands
    flat = signal_ref[...].reshape(band * quarter, lon_count)
    base = pl.program_id(0) * band
    trig = trig_ref[:, first_row:first_row + rows, :].reshape(4 * rows, lon_count)
    spectrum = lax.dot_general(flat, trig, (((1,), (1,)), ((), ())), preferred_element_type=F32)
    for j in range(band):
        piece = (spectrum[j * quarter:(j + 1) * quarter] * weight_ref[base + j]).astype(BF16).T
        held_ref[j] = jnp.concatenate([piece[q * rows:(q + 1) * rows] for q in range(4)], axis=1)
    first = 0
    for out_ref, count in zip(outs, counts):
        for at in range(0, count * bands, BAND):
            block = held_ref[:, first + at:first + at + BAND, :].reshape(band * BAND, lanes)
            turned = jnp.dot(swap_ref[...], block, preferred_element_type=F32).astype(BF16)
            for r in range(BAND):
                g, k = divmod(at + r, bands)
                out_ref[k, g] = turned[r * band:(r + 1) * band]
        first += count * bands


def forward_rows(signal, trig, weight, swap, first_row, counts, lat_count, cost, after=()):
    lat_rows, quarter, lon_count = signal.shape
    rows = sum(counts) * lat_count
    lanes = 4 * quarter
    spec = pltpu.PrefetchScalarGridSpec(
        num_scalar_prefetch=1,
        grid=(lat_rows // BAND,),
        in_specs=[
            pl.BlockSpec((BAND, quarter, lon_count), lambda i, w: (i, 0, 0)),
            pl.BlockSpec(trig.shape, lambda i, w: (0, 0, 0)),
            pl.BlockSpec(swap.shape, lambda i, w: (0, 0)),
        ]
        + [HELD] * len(after),
        out_specs=[pl.BlockSpec((lat_count, n, BAND, lanes), lambda i, w: (0, 0, i, 0)) for n in counts],
        scratch_shapes=[pltpu.VMEM((BAND, rows, lanes), BF16)],
    )
    return pl.pallas_call(
        functools.partial(forward_body, first_row, counts),
        grid_spec=spec,
        out_shape=[jax.ShapeDtypeStruct((lat_count, n, lat_rows, lanes), BF16) for n in counts],
        compiler_params=params(),
        cost_estimate=cost,
        name="forward_rows",
    )(weight, signal, trig, swap, *after)


def inverse_body(counts, synth_ref, swap_ref, *refs):
    ins, out_ref, held_ref, turned_ref = refs[:-3], refs[-3], refs[-2], refs[-1]
    band, quarter, lon_count = out_ref.shape
    bands = ins[0].shape[0]
    lanes = held_ref.shape[-1]
    first = 0
    for part, count in zip(ins, counts):
        for at in range(0, count * bands, BAND):
            tiles = [part[(at + r) % bands, (at + r) // bands] for r in range(BAND)]
            block = jnp.concatenate(tiles, axis=0)
            turned = jnp.dot(swap_ref[...], block, preferred_element_type=F32).astype(BF16)
            held_ref[:, first + at:first + at + BAND, :] = turned.reshape(band, BAND, lanes)
        first += count * bands

    @pl.loop(0, band, unroll=4)
    def _(j):
        across = held_ref[j].T
        turned_ref[j] = jnp.concatenate(
            [across[q * quarter:(q + 1) * quarter] for q in range(4)], axis=1
        )

    split = 4
    @pl.loop(0, band // split)
    def _(block):
        at = block * split
        left = turned_ref[pl.ds(at, split)].reshape(split * quarter, turned_ref.shape[-1])
        total = jnp.dot(left, synth_ref[...], preferred_element_type=F32)
        out_ref[pl.ds(at, split)] = total.astype(out_ref.dtype).reshape(split, quarter, lon_count)


def inverse_rows(parts, synth, swap, lat_rows, quarter):
    lat_count = parts[0].shape[0]
    counts = [p.shape[1] for p in parts]
    rows = synth.shape[1]
    lon_count = synth.shape[2]
    lanes = 4 * quarter
    synth = synth.reshape(4 * rows, lon_count)
    return pl.pallas_call(
        functools.partial(inverse_body, counts),
        grid=(lat_rows // BAND,),
        in_specs=[
            pl.BlockSpec(synth.shape, lambda i: (0, 0)),
            pl.BlockSpec(swap.shape, lambda i: (0, 0)),
        ]
        + [pl.BlockSpec((lat_count, n, BAND, lanes), lambda i: (0, 0, i, 0)) for n in counts],
        out_specs=pl.BlockSpec((BAND, quarter, lon_count), lambda i: (i, 0, 0)),
        out_shape=jax.ShapeDtypeStruct((lat_rows, quarter, lon_count), BF16),
        scratch_shapes=[
            pltpu.VMEM((BAND, rows, lanes), BF16),
            pltpu.VMEM((BAND, quarter, 4 * rows), BF16),
        ],
        compiler_params=params(),
        cost_estimate=LIGHT,
        name="inverse_rows",
    )(synth, swap, *parts)


def synthesise_body(plan, count_ref, chan_ref, table_ref, lanes_ref, *refs):
    chan_count = plan["chans"]
    ins, out_ref, packed = refs[:chan_count], refs[-2], refs[-1]
    step = pl.program_id(0)
    depth = table_ref.shape[0]
    lat_total = table_ref.shape[1] // 2
    part = plan["part"]

    @pl.when(step == 0)
    def _():
        for shift, part_ref in enumerate(ins):
            owner = lax.rem(chan_ref[0] + (chan_count - shift), chan_count)
            at = pl.multiple_of(plan["pad"] + owner * part, STEP)
            packed[pl.ds(at, part), :] = part_ref[...]

    start = pl.multiple_of(count_ref[0, step], STEP)
    below = count_ref[1, step]
    rows = packed[pl.ds(start, depth), :]
    held = lax.broadcasted_iota(jnp.int32, rows.shape, 0) >= below
    rows = by_parity(jnp.where(held, rows, jnp.zeros_like(rows)), lanes_ref)
    table = jnp.concatenate([table_ref[:, :lat_total], table_ref[:, lat_total:]], axis=0)
    both = lax.dot_general(table, rows, (((0,), (0,)), ((), ())), preferred_element_type=F32)
    out_ref[...] = both.astype(out_ref.dtype).reshape(out_ref.shape)


def synthesise(plan, chan, table, parts, bands, after=()):
    _, depth, lat_wide = table.shape
    count = len(plan["groups"])
    chan_count = len(parts)
    part, lanes = parts[0].shape
    lat_total = lat_wide // 2
    band_rows = lat_total // bands
    numbers = jnp.asarray(np.array([plan["starts"], plan["skips"]], np.int32))
    spec = pltpu.PrefetchScalarGridSpec(
        num_scalar_prefetch=2,
        grid=(count,),
        in_specs=[
            pl.BlockSpec((None, depth, lat_wide), lambda i, s, c: (i, 0, 0)),
            pl.BlockSpec((2, lanes), lambda i, s, c: (0, 0)),
        ]
        + [pl.BlockSpec((part, lanes), lambda i, s, c: (0, 0))] * chan_count
        + [HELD] * len(after),
        out_specs=pl.BlockSpec((bands, None, band_rows, lanes), lambda i, s, c: (0, i, 0, 0)),
        scratch_shapes=[pltpu.VMEM((plan["pad"] + plan["total"], lanes), BF16)],
    )
    return pl.pallas_call(
        functools.partial(synthesise_body, plan),
        grid_spec=spec,
        out_shape=jax.ShapeDtypeStruct((bands, count, band_rows, lanes), BF16),
        compiler_params=params(),
        cost_estimate=HEAVY,
        name="synthesise",
    )(numbers, chan, table, parity_lanes(lanes), *parts, *after)


def split_groups(group_count, even):
    few = max(even, group_count // 6 // even * even)
    first = list(range(few))
    last = list(range(few, 2 * few))
    rest = list(range(2 * few, group_count))
    half = len(rest) * 5 // 8 // even * even
    return [p for p in (first, rest[:half], rest[half:], last) if p]


def on_device(signal, spectral_filter, channel_mix):
    lat_count = lax.axis_size("lat")
    chan_count = lax.axis_size("chan")
    lat_rows, quarter, lon_count = signal.shape
    lat_total = lat_rows * lat_count
    degrees = spectral_filter.shape[0]
    group_rows = 2 * lat_count
    group_count = degrees // group_rows
    lat_index = lax.axis_index("lat")
    chan_index = lax.axis_index("chan")
    chan = jnp.reshape(chan_index, (1,)).astype(jnp.int32)
    lanes = 4 * quarter

    kernels = lat_rows % BAND == 0 and quarter % BAND == 0 and (2 * lat_count) % BAND == 0 and group_count % 2 == 0
    pieces = split_groups(group_count, 2 if kernels else 1)

    e_at = jnp.arange(2, dtype=jnp.int32)
    group_orders = jnp.asarray(np.array([group_rows * g for p in pieces for g in p], np.int32))
    trig, synth = fourier_tables(group_orders, lat_count, lon_count)
    own_rows = lat_index * lat_rows + jnp.arange(lat_rows, dtype=jnp.int32)
    _, _, own_weight = latitude_terms(own_rows, lat_total, lon_count)
    cosine, log_sine, _ = latitude_terms(jnp.arange(lat_total, dtype=jnp.int32), lat_total, lon_count)
    orders_own = (group_orders[:, None] + 2 * lat_index + e_at[None, :]).reshape(-1)
    seeds = seed_logs(orders_own, log_sine)
    swap = swap_matrix()

    gains = lax.dynamic_slice_in_dim(spectral_filter, chan_index * quarter, quarter, 2)
    direct = jnp.tile(gains[:, 0, :], (1, 4))
    cross = jnp.concatenate([jnp.tile(-gains[:, 1, :], (1, 2)), jnp.tile(gains[:, 1, :], (1, 2))], 1)

    last_moved = [None] * chan_count

    def moved(parts):
        out = [parts[0]]
        for shift in range(1, chan_count):
            pairs = [(i, (i + shift) % chan_count) for i in range(chan_count)]
            part = parts[shift]
            if last_moved[shift] is not None:
                part = lax.optimization_barrier((part, last_moved[shift]))[0]
            last_moved[shift] = lax.ppermute(part, "chan", pairs)
            out.append(last_moved[shift])
        return out

    plans = [chunk_plan(groups, group_rows, degrees, chan_count) for groups in pieces]
    counts = [len(groups) for groups in pieces]
    edges = [sum(counts[:i]) for i in range(len(counts))]
    latest = [None]

    def queued(op, *args):
        held = tuple(x for x in latest if x is not None)
        del latest[1:]
        out = op(*args, after=held)
        latest[0] = out[0] if isinstance(out, (list, tuple)) else out
        return out

    chunks = len(plans)
    spectra, exchanged, tables, filtered, mixed, returned = {}, {}, {}, {}, {}, {}
    last_exchange = [None]

    def across_lat(x, *after):
        held = [a for a in after + (last_exchange[0],) if a is not None]
        if held:
            x = lax.optimization_barrier((x, *held))[0]
        last_exchange[0] = lax.all_to_all(x, "lat", split_axis=0, concat_axis=0, tiled=True)
        return last_exchange[0]

    def do_forward(which, cost):
        if kernels:
            first = edges[which[0]] * lat_count
            made = queued(
                forward_rows, signal, trig, own_weight, swap, first, [counts[i] for i in which],
                lat_count, cost
            )
            for i, out in zip(which, made):
                spectra[i] = out
            return
        for i in which:
            part = trig.reshape(4, group_count, lat_count, lon_count)[:, edges[i]:edges[i] + counts[i]]
            spectrum = jnp.einsum("jcn,qgkn->kgjqc", signal, part, preferred_element_type=F32)
            spectrum = (spectrum * own_weight[None, None, :, None, None]).astype(BF16)
            spectra[i] = spectrum.reshape(lat_count, counts[i], lat_rows, lanes)

    def do_exchange(i):
        exchanged[i] = across_lat(spectra[i])

    def do_table(i):
        own = slice(2 * edges[i], 2 * (edges[i] + counts[i]))
        tables[i] = queued(
            legendre_table, plans[i], seeds[own], orders_own[own].astype(F32), cosine, degrees
        )

    def do_analyse(i):
        filtered[i] = moved(queued(analyse, plans[i], chan, exchanged[i], tables[i], direct, cross, chan_count))

    def do_mix(i):
        mixed[i] = moved(queued(mix, chan, filtered[i], kernel))

    def do_synthesise(i):
        back = queued(synthesise, plans[i], chan, tables[i], mixed[i], lat_count)
        returned[i] = across_lat(back)

    do_forward([0, 1], LIGHT)
    do_exchange(0)
    do_table(0)
    do_analyse(0)
    do_exchange(1)
    kernel = queued(mix_kernel, channel_mix, chan_count)
    last = chunks - 1
    for i in range(1, chunks):
        do_table(i)
        do_analyse(i)
        if 1 < i < last:
            do_exchange(i + 1)
        if i == 1:
            do_forward(list(range(2, chunks)), HEAVY)
            do_exchange(2)
        if i <= 2:
            do_mix(i - 1)
    for i in range(max(chunks - 2, 0)):
        do_synthesise(i)
    for i in range(max(chunks - 2, 0), chunks):
        if i == last - 1 and i - 2 in returned:
            latest.append(returned[i - 2])
        if i not in mixed:
            do_mix(i)
    for i in range(max(chunks - 2, 0), chunks):
        if i == last - 1 and i - 1 in returned:
            latest.append(returned[i - 1])
        do_synthesise(i)
    returned = [returned[i] for i in range(chunks)]
    if kernels:
        return inverse_rows(returned, synth, swap, lat_rows, quarter)
    rows = jnp.concatenate(returned, 1).reshape(lat_count, group_count, lat_rows, 4, quarter)
    synth = synth.reshape(4, group_count, lat_count, lon_count)
    output = jnp.einsum("kgjqd,qgkn->jdn", rows, synth, preferred_element_type=F32)
    return output.astype(BF16)


def solution(mesh):
    return jax.shard_map(
        on_device,
        mesh=mesh,
        in_specs=(P("lat", "chan", None), P(), P()),
        out_specs=P("lat", "chan", None),
        check_vma=False,
    )
```

```python
import functools
import math

import jax
import jax.numpy as jnp
import numpy as np
from jax import lax
from jax.experimental import pallas as pl
from jax.experimental.pallas import tpu as pltpu
from jax.sharding import PartitionSpec as P

F32 = jnp.float32
BF16 = jnp.bfloat16
VMEM_BYTES = 56 << 20
STEP = 16
HELD = pl.BlockSpec(memory_space=pl.ANY)
LIGHT = pl.CostEstimate(flops=1000, transcendentals=0, bytes_accessed=1000)
MEDIUM = pl.CostEstimate(flops=10_000_000_000, transcendentals=0, bytes_accessed=1000)
HEAVY = pl.CostEstimate(flops=200_000_000_000, transcendentals=0, bytes_accessed=1000)


def params(**kw):
    return pltpu.CompilerParams(vmem_limit_bytes=VMEM_BYTES, **kw)


def turns(orders, lon_count):
    cells = jnp.arange(lon_count, dtype=jnp.int32)
    phase = orders[:, None] * cells[None, :] % lon_count
    angle = phase.astype(F32) * (2.0 * math.pi / lon_count)
    return jnp.cos(angle), jnp.sin(angle)


def fourier_tables(group_orders, lat_count, lon_count):
    cos_g, sin_g = turns(group_orders, lon_count)
    fine = jnp.arange(2, dtype=jnp.int32)[:, None] + 2 * jnp.arange(lat_count, dtype=jnp.int32)[None, :]
    cos_f, sin_f = turns(fine.reshape(-1), lon_count)
    cos_g, sin_g, cos_f, sin_f = lax.optimization_barrier((cos_g, sin_g, cos_f, sin_f))
    cos_g, sin_g = cos_g[None, :, None, :], sin_g[None, :, None, :]
    cos_f = cos_f.reshape(2, 1, lat_count, lon_count)
    sin_f = sin_f.reshape(2, 1, lat_count, lon_count)
    forward = jnp.stack([cos_g * cos_f - sin_g * sin_f, -(sin_g * cos_f + cos_g * sin_f)], 0)
    orders = group_orders[None, :, None] + fine[:, None, :]
    factor = jnp.where(orders == 0, 1.0, 2.0).astype(F32)[None, :, :, :, None]
    shape = (4, group_orders.shape[0] * lat_count, lon_count)
    return (forward.astype(BF16).reshape(shape), (forward * factor).astype(BF16).reshape(shape))


def latitude_terms(lat_index, lat_total, lon_count):
    theta = (lat_index.astype(F32) + 0.5) * (math.pi / lat_total)
    weight = jnp.sin(theta) * (2.0 * math.pi * math.pi / (lat_total * lon_count))
    return (jnp.cos(theta), jnp.log(jnp.sin(theta)), weight)


def seed_logs(orders, log_sine):
    order_f = orders.astype(F32)[:, None]
    base_term = 0.5 * jnp.log((2.0 * order_f + 1.0) / (4.0 * math.pi))
    ratio_term = 0.5 * (
        jax.scipy.special.gammaln(order_f + 0.5)
        - jax.scipy.special.gammaln(order_f + 1.0)
        - 0.5 * math.log(math.pi)
    )
    return base_term + ratio_term + order_f * log_sine[None, :]


def table_body(group_rows, first_group, base, inverse_ref, seeds_ref, order_ref, cosine_ref, swap_ref, *refs):
    out_ref, rows_ref = refs[-2:]
    depth = out_ref.shape[1]
    slots, lat_total = seeds_ref.shape
    per_step = slots // 2
    first = (first_group + pl.program_id(0) * per_step) * group_rows - base
    first_block = first // STEP
    blank = jnp.zeros((STEP, 2 * lat_total), out_ref.dtype)

    @pl.loop(0, first_block)
    def _(block):
        at = pl.multiple_of(block * STEP, STEP)
        for group in range(per_step):
            out_ref[group, pl.ds(at, STEP), :] = blank

    order = order_ref[...]
    order_sq = order * order
    cosine = jnp.broadcast_to(cosine_ref[...], (slots, lat_total))
    wide = lat_total // 128

    def spread(x):
        return jnp.concatenate([x] * wide, axis=1)

    seeds = seeds_ref[...]
    zero = jnp.zeros((slots, lat_total), F32)
    start = (zero, zero, seeds, jnp.zeros((slots, 128), F32))

    def advance(block, carry):
        fresh, before, log_scale, coeff_b = carry
        at = pl.multiple_of(block * STEP, STEP)
        scale = jnp.exp(log_scale)
        for step in range(STEP):
            degree = base + at + step
            degree_v = jnp.full((slots, 128), degree.astype(F32), F32)
            ratio = jnp.maximum(degree_v * degree_v - order_sq, 1.0) * inverse_ref[degree]
            root = lax.rsqrt(ratio)
            root = root * (1.5 - 0.5 * ratio * root * root)
            starts = jnp.where(degree_v == order, 1.0, 0.0)
            grown = spread(root) * (cosine * fresh - spread(coeff_b) * before) + spread(starts)
            coeff_b = ratio * root
            before, fresh = fresh, grown
            rows_ref[step] = (grown * scale).astype(rows_ref.dtype)
        size = jnp.abs(fresh) + jnp.abs(before)
        size = jnp.where(size == 0.0, 1.0, size)
        inverse = 1.0 / size
        if slots == STEP:
            rows = rows_ref[...].reshape(STEP * slots, lat_total)
            turned = jnp.dot(swap_ref[...], rows, preferred_element_type=F32).astype(out_ref.dtype)
        for slot in range(slots):
            cut = slice((slot % 2) * lat_total, (slot % 2 + 1) * lat_total)
            made = turned[slot * STEP:(slot + 1) * STEP] if slots == STEP else rows_ref[:, slot, :]
            out_ref[slot // 2, pl.ds(at, STEP), cut] = made.astype(out_ref.dtype)
        return (fresh * inverse, before * inverse, log_scale + jnp.log(size), coeff_b)

    lax.fori_loop(first_block, depth // STEP, advance, start)


def legendre_table(all_groups, group_rows, seeds, orders_f, cosine, degrees, cost, after=()):
    order_count, lat_total = seeds.shape
    groups = order_count // 2
    per_step = max(n for n in range(1, 9) if groups % n == 0)
    slots = 2 * per_step
    base = group_rows * all_groups[0]
    depth = degrees - base
    order_wide = jnp.broadcast_to(orders_f[:, None], (order_count, 128))
    steps = groups // per_step
    seeds = seeds.reshape(steps, slots, lat_total)
    order_wide = order_wide.reshape(steps, slots, 128)
    at = np.arange(degrees, dtype=np.float32)
    inverse = jnp.asarray((1.0 / np.maximum(4.0 * at * at - 1.0, 1.0)).astype(np.float32))
    spec = pltpu.PrefetchScalarGridSpec(
        num_scalar_prefetch=1,
        grid=(steps,),
        in_specs=[
            pl.BlockSpec((None, slots, lat_total), lambda i, v: (i, 0, 0)),
            pl.BlockSpec((None, slots, 128), lambda i, v: (i, 0, 0)),
            pl.BlockSpec((1, lat_total), lambda i, v: (0, 0)),
            pl.BlockSpec((STEP * STEP, STEP * STEP), lambda i, v: (0, 0)),
        ]
        + [HELD] * len(after),
        out_specs=pl.BlockSpec((per_step, depth, 2 * lat_total), lambda i, v: (i, 0, 0)),
        scratch_shapes=[pltpu.VMEM((STEP, slots, lat_total), BF16 if slots == STEP else F32)],
    )
    return pl.pallas_call(
        functools.partial(table_body, group_rows, all_groups[0], base),
        grid_spec=spec,
        out_shape=jax.ShapeDtypeStruct((groups, depth, 2 * lat_total), BF16),
        compiler_params=params(),
        cost_estimate=cost,
        name="legendre_table",
    )(inverse, seeds, order_wide, cosine[None, :], swap_matrix(), *after)


def parity_lanes(lanes):
    second = (np.arange(lanes) % (lanes // 2)) >= lanes // 4
    return jnp.asarray(np.stack([1.0 - second, second]).astype(np.float32)).astype(BF16)


def by_parity(rows, lanes_ref):
    return jnp.concatenate([rows * lanes_ref[0:1, :], rows * lanes_ref[1:2, :]], axis=0)


def analyse_body(plan, count_ref, chan_ref, fourier_ref, table_ref, gain_ref, cross_ref, lanes_ref, *refs):
    outs, packed = refs[-1 - plan["chans"]:-1], refs[-1]
    step = pl.program_id(0)
    depth = table_ref.shape[0]
    lat_total = table_ref.shape[1] // 2
    lanes = fourier_ref.shape[-1]
    part = plan["part"]
    base = plan["base"]
    start = pl.multiple_of(count_ref[step], STEP)

    @pl.when(step == 0)
    def _():
        tail = plan["pad"] + plan["rows"]
        left = packed.shape[0] - tail
        if left:
            packed[tail:, :] = jnp.zeros((left, lanes), packed.dtype)

    rows_in = by_parity(fourier_ref[...].reshape(lat_total, lanes), lanes_ref)
    both = jnp.dot(table_ref[...], rows_in, preferred_element_type=F32)
    swapped = pltpu.roll(both, lanes // 2, 1)
    kept = both * gain_ref[base:, :] + swapped * cross_ref[base:, :]
    packed[pl.ds(start, depth), :] = kept.astype(packed.dtype)

    @pl.when(step == pl.num_programs(0) - 1)
    def _():
        for shift, out in enumerate(outs):
            owner = lax.rem(chan_ref[0] + shift, len(outs))
            at = pl.multiple_of(plan["pad"] + owner * part, STEP)
            out[...] = packed[pl.ds(at, part), :]


def chunk_plan(groups, group_rows, degrees, chan_count):
    sizes = [degrees - group_rows * g for g in groups]
    offsets = [sum(sizes[:i]) for i in range(len(groups))]
    rows = sum(sizes)
    unit = STEP * chan_count
    total = -(-rows // unit) * unit
    base = group_rows * groups[0]
    skips = [group_rows * g - base for g in groups]
    pad = max([skip - o for skip, o in zip(skips, offsets)] + [0])
    pad = -(-pad // STEP) * STEP
    starts = [pad + o - skip for skip, o in zip(skips, offsets)]
    return {
        "base": base, "skips": skips, "group_rows": group_rows, "chans": chan_count,
        "groups": groups, "rows": rows, "total": total, "part": total // chan_count,
        "pad": pad, "starts": starts,
    }


def analyse(plan, chan, fourier, table, gain, cross, chan_count, cost, after=()):
    bands, count, band_rows, lanes = fourier.shape
    table, first, row = table
    _, whole, lat_wide = table.shape
    depth = whole - row
    starts = jnp.asarray(np.array(plan["starts"][::-1], np.int32))
    spec = pltpu.PrefetchScalarGridSpec(
        num_scalar_prefetch=2,
        grid=(count,),
        in_specs=[
            pl.BlockSpec((bands, None, band_rows, lanes), lambda i, s, c: (0, count - 1 - i, 0, 0)),
            pl.BlockSpec((None, pl.Element(depth), pl.Element(lat_wide)), lambda i, s, c: (first + count - 1 - i, row, 0)),
            pl.BlockSpec(gain.shape, lambda i, s, c: (0, 0)),
            pl.BlockSpec(cross.shape, lambda i, s, c: (0, 0)),
            pl.BlockSpec((2, lanes), lambda i, s, c: (0, 0)),
        ]
        + [HELD] * len(after),
        out_specs=[pl.BlockSpec((plan["part"], lanes), lambda i, s, c: (0, 0))] * chan_count,
        scratch_shapes=[pltpu.VMEM((plan["pad"] + plan["total"], lanes), BF16)],
    )
    return pl.pallas_call(
        functools.partial(analyse_body, plan),
        grid_spec=spec,
        out_shape=[jax.ShapeDtypeStruct((plan["part"], lanes), BF16)] * chan_count,
        compiler_params=params(),
        cost_estimate=cost,
        name="analyse",
    )(starts, chan, fourier, table, gain, cross, parity_lanes(lanes), *after)


def gain_body(chan_ref, filter_ref, direct_ref, cross_ref):
    quarter = direct_ref.shape[1] // 4
    channels = filter_ref.shape[1] // 2
    for q in range(channels // quarter):
        @pl.when(chan_ref[0] == q)
        def _():
            real = filter_ref[:, q * quarter:(q + 1) * quarter]
            imag = filter_ref[:, channels + q * quarter:channels + (q + 1) * quarter]
            direct_ref[...] = jnp.concatenate([real] * 4, axis=1)
            cross_ref[...] = jnp.concatenate([-imag, -imag, imag, imag], axis=1)


def gain_tables(spectral_filter, chan, quarter):
    degrees = spectral_filter.shape[0]
    table = jax.ShapeDtypeStruct((degrees, 4 * quarter), F32)
    spec = pltpu.PrefetchScalarGridSpec(
        num_scalar_prefetch=1,
        grid=(1,),
        in_specs=[pl.BlockSpec(spectral_filter.shape, lambda i, c: (0, 0))],
        out_specs=[pl.BlockSpec(table.shape, lambda i, c: (0, 0))] * 2,
    )
    return pl.pallas_call(
        gain_body,
        grid_spec=spec,
        out_shape=[table] * 2,
        compiler_params=params(),
        cost_estimate=LIGHT,
        name="gain_tables",
    )(chan, spectral_filter)


def kernel_body(mix_ref, *refs):
    out_ref = refs[-1]
    real, imag = mix_ref[0], mix_ref[1]
    quarter = real.shape[0]
    table = [[real, imag], [-imag, real]]
    for target in range(out_ref.shape[0]):
        cut = slice(target * quarter, (target + 1) * quarter)
        for t in range(2):
            row = [table[t][u][:, cut] for u in range(2)]
            out_ref[target, t * quarter:(t + 1) * quarter, :] = jnp.concatenate(row, axis=1)


def mix_kernel(channel_mix, chan_count, after=()):
    channels = channel_mix.shape[1]
    quarter = channels // chan_count
    wide = 2 * quarter
    return pl.pallas_call(
        kernel_body,
        grid=(chan_count,),
        in_specs=[pl.BlockSpec((2, quarter, channels), lambda i: (0, i, 0))] + [HELD] * len(after),
        out_specs=pl.BlockSpec((None, chan_count, wide, wide), lambda i: (i, 0, 0, 0)),
        out_shape=jax.ShapeDtypeStruct((chan_count, chan_count, wide, wide), BF16),
        compiler_params=params(),
        cost_estimate=HEAVY,
        name="mix_kernel",
    )(channel_mix, *after)


def mix_body(chan_count, chan_ref, *refs):
    ins, kernel_ref, outs = refs[:chan_count], refs[chan_count], refs[-chan_count:]
    own = chan_ref[0]
    quarter = ins[0].shape[1] // 4
    sources = [lax.rem(own + (chan_count - back), chan_count) for back in range(chan_count)]
    left = []
    for e in range(2):
        pieces = []
        for part in ins:
            for t in range(2):
                at = (2 * t + e) * quarter
                pieces.append(part[:, at:at + quarter])
        left.append(jnp.concatenate(pieces, axis=1))
    for shift, out in enumerate(outs):
        target = lax.rem(own + shift, chan_count)
        right = jnp.concatenate([kernel_ref[source, target] for source in sources], axis=0)
        made = [jnp.dot(x, right, preferred_element_type=F32).astype(out.dtype) for x in left]
        out[...] = jnp.concatenate(
            [made[e][:, u * quarter:(u + 1) * quarter] for u in range(2) for e in range(2)], axis=1
        )


def mix(chan, parts, kernel, cost, after=()):
    chan_count = len(parts)
    rows, lanes = parts[0].shape
    spec = pltpu.PrefetchScalarGridSpec(
        num_scalar_prefetch=1,
        grid=(1,),
        in_specs=[pl.BlockSpec((rows, lanes), lambda i, c: (0, 0))] * chan_count
        + [pl.BlockSpec(kernel.shape, lambda i, c: (0, 0, 0, 0))]
        + [HELD] * len(after),
        out_specs=[pl.BlockSpec((rows, lanes), lambda i, c: (0, 0))] * chan_count,
    )
    return pl.pallas_call(
        functools.partial(mix_body, chan_count),
        grid_spec=spec,
        out_shape=[jax.ShapeDtypeStruct((rows, lanes), BF16)] * chan_count,
        compiler_params=params(),
        cost_estimate=cost,
        name="mix",
    )(chan, *parts, kernel, *after)


BAND = 16


def swap_matrix():
    at = np.arange(BAND * BAND)
    turned = (at % BAND) * BAND + at // BAND
    return jnp.asarray(np.eye(BAND * BAND, dtype=np.float32)[turned]).astype(BF16)


def forward_body(first_row, counts, weight_ref, signal_ref, trig_ref, swap_ref, *refs):
    outs, held_ref = refs[-1 - len(counts):-1], refs[-1]
    band, quarter, lon_count = signal_ref.shape
    bands = outs[0].shape[0]
    lanes = outs[0].shape[-1]
    rows = sum(counts) * bands
    flat = signal_ref[...].reshape(band * quarter, lon_count)
    base = pl.program_id(0) * band
    trig = trig_ref[:, first_row:first_row + rows, :].reshape(4 * rows, lon_count)
    spectrum = lax.dot_general(flat, trig, (((1,), (1,)), ((), ())), preferred_element_type=F32)
    for j in range(band):
        piece = (spectrum[j * quarter:(j + 1) * quarter] * weight_ref[base + j]).astype(BF16).T
        held_ref[j] = jnp.concatenate([piece[q * rows:(q + 1) * rows] for q in range(4)], axis=1)
    first = 0
    for out_ref, count in zip(outs, counts):
        for at in range(0, count * bands, BAND):
            block = held_ref[:, first + at:first + at + BAND, :].reshape(band * BAND, lanes)
            turned = jnp.dot(swap_ref[...], block, preferred_element_type=F32).astype(BF16)
            for r in range(BAND):
                g, k = divmod(at + r, bands)
                out_ref[k, g] = turned[r * band:(r + 1) * band]
        first += count * bands


def forward_rows(signal, trig, weight, swap, first_row, counts, lat_count, cost, after=()):
    lat_rows, quarter, lon_count = signal.shape
    rows = sum(counts) * lat_count
    lanes = 4 * quarter
    spec = pltpu.PrefetchScalarGridSpec(
        num_scalar_prefetch=1,
        grid=(lat_rows // BAND,),
        in_specs=[
            pl.BlockSpec((BAND, quarter, lon_count), lambda i, w: (i, 0, 0)),
            pl.BlockSpec(trig.shape, lambda i, w: (0, 0, 0)),
            pl.BlockSpec(swap.shape, lambda i, w: (0, 0)),
        ]
        + [HELD] * len(after),
        out_specs=[pl.BlockSpec((lat_count, n, BAND, lanes), lambda i, w: (0, 0, i, 0)) for n in counts],
        scratch_shapes=[pltpu.VMEM((BAND, rows, lanes), BF16)],
    )
    return pl.pallas_call(
        functools.partial(forward_body, first_row, counts),
        grid_spec=spec,
        out_shape=[jax.ShapeDtypeStruct((lat_count, n, lat_rows, lanes), BF16) for n in counts],
        compiler_params=params(),
        cost_estimate=cost,
        name="forward_rows",
    )(weight, signal, trig, swap, *after)


def turn_rows(counts, swap_ref, ins, held_ref, turned_ref):
    band, quarter, _ = turned_ref.shape
    bands = ins[0].shape[0]
    lanes = held_ref.shape[-1]
    first = 0
    for part, count in zip(ins, counts):
        for at in range(0, count * bands, BAND):
            tiles = [part[(at + r) % bands, (at + r) // bands] for r in range(BAND)]
            block = jnp.concatenate(tiles, axis=0)
            turned = jnp.dot(swap_ref[...], block, preferred_element_type=F32).astype(BF16)
            held_ref[:, first + at:first + at + BAND, :] = turned.reshape(band, BAND, lanes)
        first += count * bands

    @pl.loop(0, band, unroll=4)
    def _(j):
        across = held_ref[j].T
        turned_ref[j] = jnp.concatenate(
            [across[q * quarter:(q + 1) * quarter] for q in range(4)], axis=1
        )


def early_body(counts, swap_ref, *refs):
    turn_rows(counts, swap_ref, refs[:-2], refs[-1], refs[-2])


def early_rows(parts, swap, lat_rows, quarter):
    lat_count = parts[0].shape[0]
    counts = [p.shape[1] for p in parts]
    rows = sum(counts) * lat_count
    lanes = 4 * quarter
    return pl.pallas_call(
        functools.partial(early_body, counts),
        grid=(lat_rows // BAND,),
        in_specs=[pl.BlockSpec(swap.shape, lambda i: (0, 0))]
        + [pl.BlockSpec((lat_count, n, BAND, lanes), lambda i: (0, 0, i, 0)) for n in counts],
        out_specs=pl.BlockSpec((BAND, quarter, 4 * rows), lambda i: (i, 0, 0)),
        out_shape=jax.ShapeDtypeStruct((lat_rows, quarter, 4 * rows), BF16),
        scratch_shapes=[pltpu.VMEM((BAND, rows, lanes), BF16)],
        compiler_params=params(),
        cost_estimate=LIGHT,
        name="early_rows",
    )(swap, *parts)


def inverse_body(counts, synth_ref, swap_ref, early_ref, part_ref, out_ref, held_ref, turned_ref):
    band, quarter, lon_count = out_ref.shape
    turn_rows(counts, swap_ref, [part_ref], held_ref, turned_ref)
    split = 4

    @pl.loop(0, band // split)
    def _(block):
        at = block * split
        left = jnp.concatenate([early_ref[pl.ds(at, split)], turned_ref[pl.ds(at, split)]], axis=2)
        left = left.reshape(split * quarter, left.shape[-1])
        total = jnp.dot(left, synth_ref[...], preferred_element_type=F32)
        out_ref[pl.ds(at, split)] = total.astype(out_ref.dtype).reshape(split, quarter, lon_count)


def inverse_rows(early, part, synth, swap):
    lat_rows, quarter, wide = early.shape
    lat_count, count, _, lanes = part.shape
    rows = count * lat_count
    lon_count = synth.shape[2]
    first = wide // 4
    synth = jnp.concatenate(
        [synth[:, :first].reshape(wide, lon_count), synth[:, first:].reshape(4 * rows, lon_count)], 0
    )
    return pl.pallas_call(
        functools.partial(inverse_body, [count]),
        grid=(lat_rows // BAND,),
        in_specs=[
            pl.BlockSpec(synth.shape, lambda i: (0, 0)),
            pl.BlockSpec(swap.shape, lambda i: (0, 0)),
            pl.BlockSpec((BAND, quarter, wide), lambda i: (i, 0, 0)),
            pl.BlockSpec((lat_count, count, BAND, lanes), lambda i: (0, 0, i, 0)),
        ],
        out_specs=pl.BlockSpec((BAND, quarter, lon_count), lambda i: (i, 0, 0)),
        out_shape=jax.ShapeDtypeStruct((lat_rows, quarter, lon_count), BF16),
        scratch_shapes=[
            pltpu.VMEM((BAND, rows, lanes), BF16),
            pltpu.VMEM((BAND, quarter, 4 * rows), BF16),
        ],
        compiler_params=params(),
        cost_estimate=LIGHT,
        name="inverse_rows",
    )(synth, swap, early, part)


def synthesise_body(plan, count_ref, chan_ref, table_ref, lanes_ref, *refs):
    chan_count = plan["chans"]
    ins, out_ref, packed = refs[:chan_count], refs[-2], refs[-1]
    step = pl.program_id(0)
    depth = table_ref.shape[0]
    lat_total = table_ref.shape[1] // 2
    part = plan["part"]

    @pl.when(step == 0)
    def _():
        for shift, part_ref in enumerate(ins):
            owner = lax.rem(chan_ref[0] + (chan_count - shift), chan_count)
            at = pl.multiple_of(plan["pad"] + owner * part, STEP)
            packed[pl.ds(at, part), :] = part_ref[...]

    start = pl.multiple_of(count_ref[0, step], STEP)
    below = count_ref[1, step]
    rows = packed[pl.ds(start, depth), :]
    held = lax.broadcasted_iota(jnp.int32, rows.shape, 0) >= below
    rows = by_parity(jnp.where(held, rows, jnp.zeros_like(rows)), lanes_ref)
    table = jnp.concatenate([table_ref[:, :lat_total], table_ref[:, lat_total:]], axis=0)
    both = lax.dot_general(table, rows, (((0,), (0,)), ((), ())), preferred_element_type=F32)
    out_ref[...] = both.astype(out_ref.dtype).reshape(out_ref.shape)


def synthesise(plan, chan, table, parts, bands, cost, after=()):
    table, first, row = table
    _, whole, lat_wide = table.shape
    depth = whole - row
    count = len(plan["groups"])
    chan_count = len(parts)
    part, lanes = parts[0].shape
    lat_total = lat_wide // 2
    band_rows = lat_total // bands
    numbers = jnp.asarray(np.array([plan["starts"], plan["skips"]], np.int32))
    spec = pltpu.PrefetchScalarGridSpec(
        num_scalar_prefetch=2,
        grid=(count,),
        in_specs=[
            pl.BlockSpec((None, pl.Element(depth), pl.Element(lat_wide)), lambda i, s, c: (first + i, row, 0)),
            pl.BlockSpec((2, lanes), lambda i, s, c: (0, 0)),
        ]
        + [pl.BlockSpec((part, lanes), lambda i, s, c: (0, 0))] * chan_count
        + [HELD] * len(after),
        out_specs=pl.BlockSpec((bands, None, band_rows, lanes), lambda i, s, c: (0, i, 0, 0)),
        scratch_shapes=[pltpu.VMEM((plan["pad"] + plan["total"], lanes), BF16)],
    )
    return pl.pallas_call(
        functools.partial(synthesise_body, plan),
        grid_spec=spec,
        out_shape=jax.ShapeDtypeStruct((bands, count, band_rows, lanes), BF16),
        compiler_params=params(),
        cost_estimate=cost,
        name="synthesise",
    )(numbers, chan, table, parity_lanes(lanes), *parts, *after)


def split_groups(group_count, even):
    few = max(even, group_count // 6 // even * even)
    first = list(range(few))
    last = list(range(few, 2 * few))
    rest = list(range(2 * few, group_count))
    half = len(rest) * 5 // 8 // even * even
    return [first, rest[:half], rest[half:], last]


def on_device(signal, spectral_filter, channel_mix):
    lat_count = lax.axis_size("lat")
    chan_count = lax.axis_size("chan")
    lat_rows, quarter, lon_count = signal.shape
    lat_total = lat_rows * lat_count
    degrees = spectral_filter.shape[0]
    full_channels = channel_mix.shape[1]
    group_rows = 2 * lat_count
    group_count = degrees // group_rows
    lat_index = lax.axis_index("lat")
    chan_index = lax.axis_index("chan")
    chan = jnp.reshape(chan_index, (1,)).astype(jnp.int32)
    lanes = 4 * quarter

    kernels = lat_rows % BAND == 0 and quarter % BAND == 0 and (2 * lat_count) % BAND == 0 and group_count % 2 == 0
    pieces = split_groups(group_count, 2 if kernels else 1)

    e_at = jnp.arange(2, dtype=jnp.int32)
    group_orders = jnp.asarray(np.array([group_rows * g for p in pieces for g in p], np.int32))
    trig, synth = fourier_tables(group_orders, lat_count, lon_count)
    own_rows = lat_index * lat_rows + jnp.arange(lat_rows, dtype=jnp.int32)
    _, _, own_weight = latitude_terms(own_rows, lat_total, lon_count)
    cosine, log_sine, _ = latitude_terms(jnp.arange(lat_total, dtype=jnp.int32), lat_total, lon_count)
    orders_own = (group_orders[:, None] + 2 * lat_index + e_at[None, :]).reshape(-1)
    seeds = seed_logs(orders_own, log_sine)
    swap = swap_matrix()

    direct, cross = gain_tables(spectral_filter.reshape(degrees, 2 * full_channels), chan, quarter)

    last_moved = [None] * chan_count

    def moved(parts):
        out = [parts[0]]
        for shift in range(1, chan_count):
            pairs = [(i, (i + shift) % chan_count) for i in range(chan_count)]
            part = parts[shift]
            if last_moved[0] is not None:
                part = lax.optimization_barrier((part, last_moved[0]))[0]
            out.append(lax.ppermute(part, "chan", pairs))
        last_moved[0] = out[chan_count // 2]
        return out

    plans = [chunk_plan(groups, group_rows, degrees, chan_count) for groups in pieces]
    counts = [len(groups) for groups in pieces]
    edges = [sum(counts[:i]) for i in range(len(counts))]
    latest = [None]

    def queued(op, *args):
        held = tuple(x for x in latest if x is not None)
        del latest[1:]
        out = op(*args, after=held)
        latest[0] = out[0] if isinstance(out, (list, tuple)) else out
        return out

    chunks = len(plans)
    spectra, exchanged, tables, filtered, mixed, returned = {}, {}, {}, {}, {}, {}
    last_exchange = [None]

    def across_lat(x, *after):
        held = [a for a in after + (last_exchange[0],) if a is not None]
        if held:
            x = lax.optimization_barrier((x, *held))[0]
        last_exchange[0] = lax.all_to_all(x, "lat", split_axis=0, concat_axis=0, tiled=True)
        return last_exchange[0]

    def do_forward(which, cost):
        if kernels:
            first = edges[which[0]] * lat_count
            made = queued(
                forward_rows, signal, trig, own_weight, swap, first, [counts[i] for i in which],
                lat_count, cost
            )
            for i, out in zip(which, made):
                spectra[i] = out
            return
        for i in which:
            part = trig.reshape(4, group_count, lat_count, lon_count)[:, edges[i]:edges[i] + counts[i]]
            spectrum = jnp.einsum("jcn,qgkn->kgjqc", signal, part, preferred_element_type=F32)
            spectrum = (spectrum * own_weight[None, None, :, None, None]).astype(BF16)
            spectra[i] = spectrum.reshape(lat_count, counts[i], lat_rows, lanes)

    def do_exchange(i):
        exchanged[i] = across_lat(spectra[i])

    def do_table(which, cost):
        which = sorted(which, key=lambda i: pieces[i][0])
        joined = [g for i in which for g in pieces[i]]
        own_seeds = jnp.concatenate([seeds[2 * edges[i]:2 * (edges[i] + counts[i])] for i in which], 0)
        own_orders = jnp.concatenate([orders_own[2 * edges[i]:2 * (edges[i] + counts[i])] for i in which], 0)
        table = queued(
            legendre_table, joined, group_rows, own_seeds, own_orders.astype(F32), cosine, degrees, cost
        )
        for i in which:
            skip = pieces[i][0] - joined[0]
            tables[i] = (table, skip, skip * group_rows)

    def do_analyse(i, cost):
        filtered[i] = moved(
            queued(analyse, plans[i], chan, exchanged[i], tables[i], direct, cross, chan_count, cost)
        )

    def do_mix(i, cost):
        mixed[i] = moved(queued(mix, chan, filtered[i], kernel, cost))

    def do_synthesise(i, cost):
        back = queued(synthesise, plans[i], chan, tables[i], mixed[i], lat_count, cost)
        returned[i] = across_lat(back)

    do_forward([0, 1], LIGHT)
    do_exchange(0)
    do_table([0, 3], LIGHT)
    do_analyse(0, LIGHT)
    do_exchange(1)
    kernel = queued(mix_kernel, channel_mix, chan_count)
    do_forward([2, 3], LIGHT)
    do_mix(0, LIGHT)
    do_exchange(2)
    do_table([1, 2], HEAVY)
    do_analyse(1, LIGHT)
    do_exchange(3)
    do_synthesise(0, HEAVY)
    do_analyse(2, LIGHT)
    do_mix(1, HEAVY)
    do_analyse(3, LIGHT)
    do_synthesise(1, MEDIUM)
    do_mix(2, MEDIUM)
    do_mix(3, MEDIUM)
    do_synthesise(2, MEDIUM)
    do_synthesise(3, HEAVY)
    returned = [returned[i] for i in range(chunks)]
    if kernels:
        early = early_rows(returned[:-1], swap, lat_rows, quarter)
        return inverse_rows(early, returned[-1], synth, swap)
    rows = jnp.concatenate(returned, 1).reshape(lat_count, group_count, lat_rows, 4, quarter)
    synth = synth.reshape(4, group_count, lat_count, lon_count)
    output = jnp.einsum("kgjqd,qgkn->jdn", rows, synth, preferred_element_type=F32)
    return output.astype(BF16)


def solution(mesh):
    return jax.shard_map(
        on_device,
        mesh=mesh,
        in_specs=(P("lat", "chan", None), P(), P()),
        out_specs=P("lat", "chan", None),
        check_vma=False,
    )
```

```python
import functools
import math

import jax
import jax.numpy as jnp
import numpy as np
from jax import lax
from jax.experimental import pallas as pl
from jax.experimental.pallas import tpu as pltpu
from jax.sharding import PartitionSpec as P

F32 = jnp.float32
BF16 = jnp.bfloat16
VMEM_BYTES = 56 << 20
STEP = 16
HELD = pl.BlockSpec(memory_space=pl.ANY)
LIGHT = pl.CostEstimate(flops=1000, transcendentals=0, bytes_accessed=1000)
MEDIUM = pl.CostEstimate(flops=10_000_000_000, transcendentals=0, bytes_accessed=1000)
HEAVY = pl.CostEstimate(flops=200_000_000_000, transcendentals=0, bytes_accessed=1000)


def params(**kw):
    return pltpu.CompilerParams(vmem_limit_bytes=VMEM_BYTES, **kw)


def turns(orders, lon_count):
    cells = jnp.arange(lon_count, dtype=jnp.int32)
    phase = orders[:, None] * cells[None, :] % lon_count
    angle = phase.astype(F32) * (2.0 * math.pi / lon_count)
    return jnp.cos(angle), jnp.sin(angle)


def fourier_tables(group_orders, lat_count, lon_count):
    cos_g, sin_g = turns(group_orders, lon_count)
    fine = jnp.arange(2, dtype=jnp.int32)[:, None] + 2 * jnp.arange(lat_count, dtype=jnp.int32)[None, :]
    cos_f, sin_f = turns(fine.reshape(-1), lon_count)
    cos_g, sin_g, cos_f, sin_f = lax.optimization_barrier((cos_g, sin_g, cos_f, sin_f))
    cos_g, sin_g = cos_g[None, :, None, :], sin_g[None, :, None, :]
    cos_f = cos_f.reshape(2, 1, lat_count, lon_count)
    sin_f = sin_f.reshape(2, 1, lat_count, lon_count)
    forward = jnp.stack([cos_g * cos_f - sin_g * sin_f, -(sin_g * cos_f + cos_g * sin_f)], 0)
    orders = group_orders[None, :, None] + fine[:, None, :]
    factor = jnp.where(orders == 0, 1.0, 2.0).astype(F32)[None, :, :, :, None]
    shape = (4, group_orders.shape[0] * lat_count, lon_count)
    return (forward.astype(BF16).reshape(shape), (forward * factor).astype(BF16).reshape(shape))


def latitude_terms(lat_index, lat_total, lon_count):
    theta = (lat_index.astype(F32) + 0.5) * (math.pi / lat_total)
    weight = jnp.sin(theta) * (2.0 * math.pi * math.pi / (lat_total * lon_count))
    return (jnp.cos(theta), jnp.log(jnp.sin(theta)), weight)


def seed_logs(orders, log_sine):
    order_f = orders.astype(F32)[:, None]
    base_term = 0.5 * jnp.log((2.0 * order_f + 1.0) / (4.0 * math.pi))
    ratio_term = 0.5 * (
        jax.scipy.special.gammaln(order_f + 0.5)
        - jax.scipy.special.gammaln(order_f + 1.0)
        - 0.5 * math.log(math.pi)
    )
    return base_term + ratio_term + order_f * log_sine[None, :]


def table_body(group_rows, first_group, base, inverse_ref, seeds_ref, order_ref, cosine_ref, swap_ref, *refs):
    out_ref, rows_ref = refs[-2:]
    depth = out_ref.shape[1]
    slots, lat_total = seeds_ref.shape
    per_step = slots // 2
    first = (first_group + pl.program_id(0) * per_step) * group_rows - base
    first_block = first // STEP
    blank = jnp.zeros((STEP, 2 * lat_total), out_ref.dtype)

    @pl.loop(0, first_block)
    def _(block):
        at = pl.multiple_of(block * STEP, STEP)
        for group in range(per_step):
            out_ref[group, pl.ds(at, STEP), :] = blank

    order = order_ref[...]
    order_sq = order * order
    cosine = jnp.broadcast_to(cosine_ref[...], (slots, lat_total))
    wide = lat_total // 128

    def spread(x):
        return jnp.concatenate([x] * wide, axis=1)

    seeds = seeds_ref[...]
    zero = jnp.zeros((slots, lat_total), F32)
    start = (zero, zero, seeds, jnp.zeros((slots, 128), F32))

    def advance(block, carry):
        fresh, before, log_scale, coeff_b = carry
        at = pl.multiple_of(block * STEP, STEP)
        scale = jnp.exp(log_scale)
        for step in range(STEP):
            degree = base + at + step
            degree_v = jnp.full((slots, 128), degree.astype(F32), F32)
            ratio = jnp.maximum(degree_v * degree_v - order_sq, 1.0) * inverse_ref[degree]
            root = lax.rsqrt(ratio)
            root = root * (1.5 - 0.5 * ratio * root * root)
            starts = jnp.where(degree_v == order, 1.0, 0.0)
            grown = spread(root) * (cosine * fresh - spread(coeff_b) * before) + spread(starts)
            coeff_b = ratio * root
            before, fresh = fresh, grown
            rows_ref[step] = (grown * scale).astype(rows_ref.dtype)
        size = jnp.abs(fresh) + jnp.abs(before)
        size = jnp.where(size == 0.0, 1.0, size)
        inverse = 1.0 / size
        if slots == STEP:
            rows = rows_ref[...].reshape(STEP * slots, lat_total)
            turned = jnp.dot(swap_ref[...], rows, preferred_element_type=F32).astype(out_ref.dtype)
        for slot in range(slots):
            cut = slice((slot % 2) * lat_total, (slot % 2 + 1) * lat_total)
            made = turned[slot * STEP:(slot + 1) * STEP] if slots == STEP else rows_ref[:, slot, :]
            out_ref[slot // 2, pl.ds(at, STEP), cut] = made.astype(out_ref.dtype)
        return (fresh * inverse, before * inverse, log_scale + jnp.log(size), coeff_b)

    lax.fori_loop(first_block, depth // STEP, advance, start)


def legendre_table(all_groups, group_rows, seeds, orders_f, cosine, degrees, cost, after=()):
    order_count, lat_total = seeds.shape
    groups = order_count // 2
    per_step = max(n for n in range(1, 9) if groups % n == 0)
    slots = 2 * per_step
    base = group_rows * all_groups[0]
    depth = degrees - base
    order_wide = jnp.broadcast_to(orders_f[:, None], (order_count, 128))
    steps = groups // per_step
    seeds = seeds.reshape(steps, slots, lat_total)
    order_wide = order_wide.reshape(steps, slots, 128)
    at = np.arange(degrees, dtype=np.float32)
    inverse = jnp.asarray((1.0 / np.maximum(4.0 * at * at - 1.0, 1.0)).astype(np.float32))
    spec = pltpu.PrefetchScalarGridSpec(
        num_scalar_prefetch=1,
        grid=(steps,),
        in_specs=[
            pl.BlockSpec((None, slots, lat_total), lambda i, v: (i, 0, 0)),
            pl.BlockSpec((None, slots, 128), lambda i, v: (i, 0, 0)),
            pl.BlockSpec((1, lat_total), lambda i, v: (0, 0)),
            pl.BlockSpec((STEP * STEP, STEP * STEP), lambda i, v: (0, 0)),
        ]
        + [HELD] * len(after),
        out_specs=pl.BlockSpec((per_step, depth, 2 * lat_total), lambda i, v: (i, 0, 0)),
        scratch_shapes=[pltpu.VMEM((STEP, slots, lat_total), BF16 if slots == STEP else F32)],
    )
    return pl.pallas_call(
        functools.partial(table_body, group_rows, all_groups[0], base),
        grid_spec=spec,
        out_shape=jax.ShapeDtypeStruct((groups, depth, 2 * lat_total), BF16),
        compiler_params=params(),
        cost_estimate=cost,
        name="legendre_table",
    )(inverse, seeds, order_wide, cosine[None, :], swap_matrix(), *after)


def parity_lanes(lanes):
    second = (np.arange(lanes) % (lanes // 2)) >= lanes // 4
    return jnp.asarray(np.stack([1.0 - second, second]).astype(np.float32)).astype(BF16)


def by_parity(rows, lanes_ref):
    return jnp.concatenate([rows * lanes_ref[0:1, :], rows * lanes_ref[1:2, :]], axis=0)


def analyse_body(plan, count_ref, chan_ref, fourier_ref, table_ref, gain_ref, cross_ref, lanes_ref, *refs):
    outs, packed = refs[-1 - plan["chans"]:-1], refs[-1]
    step = pl.program_id(0)
    depth = table_ref.shape[0]
    lat_total = table_ref.shape[1] // 2
    lanes = fourier_ref.shape[-1]
    part = plan["part"]
    base = plan["base"]
    start = pl.multiple_of(count_ref[step], STEP)

    @pl.when(step == 0)
    def _():
        tail = plan["pad"] + plan["rows"]
        left = packed.shape[0] - tail
        if left:
            packed[tail:, :] = jnp.zeros((left, lanes), packed.dtype)

    rows_in = by_parity(fourier_ref[...].reshape(lat_total, lanes), lanes_ref)
    both = jnp.dot(table_ref[...], rows_in, preferred_element_type=F32)
    swapped = pltpu.roll(both, lanes // 2, 1)
    kept = both * gain_ref[base:, :] + swapped * cross_ref[base:, :]
    packed[pl.ds(start, depth), :] = kept.astype(packed.dtype)

    @pl.when(step == pl.num_programs(0) - 1)
    def _():
        for shift, out in enumerate(outs):
            owner = lax.rem(chan_ref[0] + shift, len(outs))
            at = pl.multiple_of(plan["pad"] + owner * part, STEP)
            out[...] = packed[pl.ds(at, part), :]


def chunk_plan(groups, group_rows, degrees, chan_count):
    sizes = [degrees - group_rows * g for g in groups]
    offsets = [sum(sizes[:i]) for i in range(len(groups))]
    rows = sum(sizes)
    unit = STEP * chan_count
    total = -(-rows // unit) * unit
    base = group_rows * groups[0]
    skips = [group_rows * g - base for g in groups]
    pad = max([skip - o for skip, o in zip(skips, offsets)] + [0])
    pad = -(-pad // STEP) * STEP
    starts = [pad + o - skip for skip, o in zip(skips, offsets)]
    return {
        "base": base, "skips": skips, "group_rows": group_rows, "chans": chan_count,
        "groups": groups, "rows": rows, "total": total, "part": total // chan_count,
        "pad": pad, "starts": starts,
    }


def analyse(plan, chan, fourier, table, gain, cross, chan_count, cost, after=()):
    bands, count, band_rows, lanes = fourier.shape
    table, first, row = table
    _, whole, lat_wide = table.shape
    depth = whole - row
    starts = jnp.asarray(np.array(plan["starts"][::-1], np.int32))
    spec = pltpu.PrefetchScalarGridSpec(
        num_scalar_prefetch=2,
        grid=(count,),
        in_specs=[
            pl.BlockSpec((bands, None, band_rows, lanes), lambda i, s, c: (0, count - 1 - i, 0, 0)),
            pl.BlockSpec((None, pl.Element(depth), pl.Element(lat_wide)), lambda i, s, c: (first + count - 1 - i, row, 0)),
            pl.BlockSpec(gain.shape, lambda i, s, c: (0, 0)),
            pl.BlockSpec(cross.shape, lambda i, s, c: (0, 0)),
            pl.BlockSpec((2, lanes), lambda i, s, c: (0, 0)),
        ]
        + [HELD] * len(after),
        out_specs=[pl.BlockSpec((plan["part"], lanes), lambda i, s, c: (0, 0))] * chan_count,
        scratch_shapes=[pltpu.VMEM((plan["pad"] + plan["total"], lanes), BF16)],
    )
    return pl.pallas_call(
        functools.partial(analyse_body, plan),
        grid_spec=spec,
        out_shape=[jax.ShapeDtypeStruct((plan["part"], lanes), BF16)] * chan_count,
        compiler_params=params(),
        cost_estimate=cost,
        name="analyse",
    )(starts, chan, fourier, table, gain, cross, parity_lanes(lanes), *after)


def gain_body(chan_ref, filter_ref, direct_ref, cross_ref):
    quarter = direct_ref.shape[1] // 4
    channels = filter_ref.shape[1] // 2
    for q in range(channels // quarter):
        @pl.when(chan_ref[0] == q)
        def _():
            real = filter_ref[:, q * quarter:(q + 1) * quarter]
            imag = filter_ref[:, channels + q * quarter:channels + (q + 1) * quarter]
            direct_ref[...] = jnp.concatenate([real] * 4, axis=1)
            cross_ref[...] = jnp.concatenate([-imag, -imag, imag, imag], axis=1)


def gain_tables(spectral_filter, chan, quarter):
    degrees = spectral_filter.shape[0]
    table = jax.ShapeDtypeStruct((degrees, 4 * quarter), F32)
    spec = pltpu.PrefetchScalarGridSpec(
        num_scalar_prefetch=1,
        grid=(1,),
        in_specs=[pl.BlockSpec(spectral_filter.shape, lambda i, c: (0, 0))],
        out_specs=[pl.BlockSpec(table.shape, lambda i, c: (0, 0))] * 2,
    )
    return pl.pallas_call(
        gain_body,
        grid_spec=spec,
        out_shape=[table] * 2,
        compiler_params=params(),
        cost_estimate=LIGHT,
        name="gain_tables",
    )(chan, spectral_filter)


def kernel_body(mix_ref, *refs):
    out_ref = refs[-1]
    real, imag = mix_ref[0], mix_ref[1]
    quarter = real.shape[0]
    table = [[real, imag], [-imag, real]]
    for target in range(out_ref.shape[0]):
        cut = slice(target * quarter, (target + 1) * quarter)
        for t in range(2):
            row = [table[t][u][:, cut] for u in range(2)]
            out_ref[target, t * quarter:(t + 1) * quarter, :] = jnp.concatenate(row, axis=1)


def mix_kernel(channel_mix, chan_count, after=()):
    channels = channel_mix.shape[1]
    quarter = channels // chan_count
    wide = 2 * quarter
    return pl.pallas_call(
        kernel_body,
        grid=(chan_count,),
        in_specs=[pl.BlockSpec((2, quarter, channels), lambda i: (0, i, 0))] + [HELD] * len(after),
        out_specs=pl.BlockSpec((None, chan_count, wide, wide), lambda i: (i, 0, 0, 0)),
        out_shape=jax.ShapeDtypeStruct((chan_count, chan_count, wide, wide), BF16),
        compiler_params=params(),
        cost_estimate=HEAVY,
        name="mix_kernel",
    )(channel_mix, *after)


def mix_body(chan_count, chan_ref, *refs):
    ins, kernel_ref, outs = refs[:chan_count], refs[chan_count], refs[-chan_count:]
    own = chan_ref[0]
    quarter = ins[0].shape[1] // 4
    sources = [lax.rem(own + (chan_count - back), chan_count) for back in range(chan_count)]
    left = []
    for e in range(2):
        pieces = []
        for part in ins:
            for t in range(2):
                at = (2 * t + e) * quarter
                pieces.append(part[:, at:at + quarter])
        left.append(jnp.concatenate(pieces, axis=1))
    for shift, out in enumerate(outs):
        target = lax.rem(own + shift, chan_count)
        right = jnp.concatenate([kernel_ref[source, target] for source in sources], axis=0)
        made = [jnp.dot(x, right, preferred_element_type=F32).astype(out.dtype) for x in left]
        out[...] = jnp.concatenate(
            [made[e][:, u * quarter:(u + 1) * quarter] for u in range(2) for e in range(2)], axis=1
        )


def mix(chan, parts, kernel, cost, after=()):
    chan_count = len(parts)
    rows, lanes = parts[0].shape
    spec = pltpu.PrefetchScalarGridSpec(
        num_scalar_prefetch=1,
        grid=(1,),
        in_specs=[pl.BlockSpec((rows, lanes), lambda i, c: (0, 0))] * chan_count
        + [pl.BlockSpec(kernel.shape, lambda i, c: (0, 0, 0, 0))]
        + [HELD] * len(after),
        out_specs=[pl.BlockSpec((rows, lanes), lambda i, c: (0, 0))] * chan_count,
    )
    return pl.pallas_call(
        functools.partial(mix_body, chan_count),
        grid_spec=spec,
        out_shape=[jax.ShapeDtypeStruct((rows, lanes), BF16)] * chan_count,
        compiler_params=params(),
        cost_estimate=cost,
        name="mix",
    )(chan, *parts, kernel, *after)


BAND = 16


def swap_matrix():
    at = np.arange(BAND * BAND)
    turned = (at % BAND) * BAND + at // BAND
    return jnp.asarray(np.eye(BAND * BAND, dtype=np.float32)[turned]).astype(BF16)


def forward_body(first_row, counts, weight_ref, signal_ref, trig_ref, swap_ref, *refs):
    outs, held_ref = refs[-1 - len(counts):-1], refs[-1]
    band, quarter, lon_count = signal_ref.shape
    bands = outs[0].shape[0]
    lanes = outs[0].shape[-1]
    rows = sum(counts) * bands
    flat = signal_ref[...].reshape(band * quarter, lon_count)
    base = pl.program_id(0) * band
    trig = trig_ref[:, first_row:first_row + rows, :].reshape(4 * rows, lon_count)
    spectrum = lax.dot_general(flat, trig, (((1,), (1,)), ((), ())), preferred_element_type=F32)
    for j in range(band):
        piece = (spectrum[j * quarter:(j + 1) * quarter] * weight_ref[base + j]).astype(BF16).T
        held_ref[j] = jnp.concatenate([piece[q * rows:(q + 1) * rows] for q in range(4)], axis=1)
    first = 0
    for out_ref, count in zip(outs, counts):
        for at in range(0, count * bands, BAND):
            block = held_ref[:, first + at:first + at + BAND, :].reshape(band * BAND, lanes)
            turned = jnp.dot(swap_ref[...], block, preferred_element_type=F32).astype(BF16)
            for r in range(BAND):
                g, k = divmod(at + r, bands)
                out_ref[k, g] = turned[r * band:(r + 1) * band]
        first += count * bands


def forward_rows(signal, trig, weight, swap, first_row, counts, lat_count, cost, after=()):
    lat_rows, quarter, lon_count = signal.shape
    rows = sum(counts) * lat_count
    lanes = 4 * quarter
    spec = pltpu.PrefetchScalarGridSpec(
        num_scalar_prefetch=1,
        grid=(lat_rows // BAND,),
        in_specs=[
            pl.BlockSpec((BAND, quarter, lon_count), lambda i, w: (i, 0, 0)),
            pl.BlockSpec(trig.shape, lambda i, w: (0, 0, 0)),
            pl.BlockSpec(swap.shape, lambda i, w: (0, 0)),
        ]
        + [HELD] * len(after),
        out_specs=[pl.BlockSpec((lat_count, n, BAND, lanes), lambda i, w: (0, 0, i, 0)) for n in counts],
        scratch_shapes=[pltpu.VMEM((BAND, rows, lanes), BF16)],
    )
    return pl.pallas_call(
        functools.partial(forward_body, first_row, counts),
        grid_spec=spec,
        out_shape=[jax.ShapeDtypeStruct((lat_count, n, lat_rows, lanes), BF16) for n in counts],
        compiler_params=params(),
        cost_estimate=cost,
        name="forward_rows",
    )(weight, signal, trig, swap, *after)


def turn_rows(counts, swap_ref, ins, held_ref, turned_ref):
    band, quarter, _ = turned_ref.shape
    bands = ins[0].shape[0]
    lanes = held_ref.shape[-1]
    first = 0
    for part, count in zip(ins, counts):
        for at in range(0, count * bands, BAND):
            tiles = [part[(at + r) % bands, (at + r) // bands] for r in range(BAND)]
            block = jnp.concatenate(tiles, axis=0)
            turned = jnp.dot(swap_ref[...], block, preferred_element_type=F32).astype(BF16)
            held_ref[:, first + at:first + at + BAND, :] = turned.reshape(band, BAND, lanes)
        first += count * bands

    @pl.loop(0, band, unroll=4)
    def _(j):
        across = held_ref[j].T
        turned_ref[j] = jnp.concatenate(
            [across[q * quarter:(q + 1) * quarter] for q in range(4)], axis=1
        )


def early_body(counts, swap_ref, *refs):
    turn_rows(counts, swap_ref, refs[:-2], refs[-1], refs[-2])


def early_rows(parts, swap, lat_rows, quarter):
    lat_count = parts[0].shape[0]
    counts = [p.shape[1] for p in parts]
    rows = sum(counts) * lat_count
    lanes = 4 * quarter
    return pl.pallas_call(
        functools.partial(early_body, counts),
        grid=(lat_rows // BAND,),
        in_specs=[pl.BlockSpec(swap.shape, lambda i: (0, 0))]
        + [pl.BlockSpec((lat_count, n, BAND, lanes), lambda i: (0, 0, i, 0)) for n in counts],
        out_specs=pl.BlockSpec((BAND, quarter, 4 * rows), lambda i: (i, 0, 0)),
        out_shape=jax.ShapeDtypeStruct((lat_rows, quarter, 4 * rows), BF16),
        scratch_shapes=[pltpu.VMEM((BAND, rows, lanes), BF16)],
        compiler_params=params(),
        cost_estimate=LIGHT,
        name="early_rows",
    )(swap, *parts)


def inverse_body(counts, synth_ref, swap_ref, early_ref, part_ref, out_ref, held_ref, turned_ref):
    band, quarter, lon_count = out_ref.shape
    turn_rows(counts, swap_ref, [part_ref], held_ref, turned_ref)
    split = 4

    @pl.loop(0, band // split)
    def _(block):
        at = block * split
        left = jnp.concatenate([early_ref[pl.ds(at, split)], turned_ref[pl.ds(at, split)]], axis=2)
        left = left.reshape(split * quarter, left.shape[-1])
        total = jnp.dot(left, synth_ref[...], preferred_element_type=F32)
        out_ref[pl.ds(at, split)] = total.astype(out_ref.dtype).reshape(split, quarter, lon_count)


def inverse_rows(early, part, synth, swap):
    lat_rows, quarter, wide = early.shape
    lat_count, count, _, lanes = part.shape
    rows = count * lat_count
    lon_count = synth.shape[2]
    first = wide // 4
    synth = jnp.concatenate(
        [synth[:, :first].reshape(wide, lon_count), synth[:, first:].reshape(4 * rows, lon_count)], 0
    )
    return pl.pallas_call(
        functools.partial(inverse_body, [count]),
        grid=(lat_rows // BAND,),
        in_specs=[
            pl.BlockSpec(synth.shape, lambda i: (0, 0)),
            pl.BlockSpec(swap.shape, lambda i: (0, 0)),
            pl.BlockSpec((BAND, quarter, wide), lambda i: (i, 0, 0)),
            pl.BlockSpec((lat_count, count, BAND, lanes), lambda i: (0, 0, i, 0)),
        ],
        out_specs=pl.BlockSpec((BAND, quarter, lon_count), lambda i: (i, 0, 0)),
        out_shape=jax.ShapeDtypeStruct((lat_rows, quarter, lon_count), BF16),
        scratch_shapes=[
            pltpu.VMEM((BAND, rows, lanes), BF16),
            pltpu.VMEM((BAND, quarter, 4 * rows), BF16),
        ],
        compiler_params=params(),
        cost_estimate=LIGHT,
        name="inverse_rows",
    )(synth, swap, early, part)


def synthesise_body(plan, count_ref, chan_ref, table_ref, lanes_ref, *refs):
    chan_count = plan["chans"]
    ins, out_ref, packed = refs[:chan_count], refs[-2], refs[-1]
    step = pl.program_id(0)
    depth = table_ref.shape[0]
    lat_total = table_ref.shape[1] // 2
    part = plan["part"]

    @pl.when(step == 0)
    def _():
        for shift, part_ref in enumerate(ins):
            owner = lax.rem(chan_ref[0] + (chan_count - shift), chan_count)
            at = pl.multiple_of(plan["pad"] + owner * part, STEP)
            packed[pl.ds(at, part), :] = part_ref[...]

    start = pl.multiple_of(count_ref[0, step], STEP)
    below = count_ref[1, step]
    rows = packed[pl.ds(start, depth), :]
    held = lax.broadcasted_iota(jnp.int32, rows.shape, 0) >= below
    rows = by_parity(jnp.where(held, rows, jnp.zeros_like(rows)), lanes_ref)
    table = jnp.concatenate([table_ref[:, :lat_total], table_ref[:, lat_total:]], axis=0)
    both = lax.dot_general(table, rows, (((0,), (0,)), ((), ())), preferred_element_type=F32)
    out_ref[...] = both.astype(out_ref.dtype).reshape(out_ref.shape)


def synthesise(plan, chan, table, parts, bands, cost, after=()):
    table, first, row = table
    _, whole, lat_wide = table.shape
    depth = whole - row
    count = len(plan["groups"])
    chan_count = len(parts)
    part, lanes = parts[0].shape
    lat_total = lat_wide // 2
    band_rows = lat_total // bands
    numbers = jnp.asarray(np.array([plan["starts"], plan["skips"]], np.int32))
    spec = pltpu.PrefetchScalarGridSpec(
        num_scalar_prefetch=2,
        grid=(count,),
        in_specs=[
            pl.BlockSpec((None, pl.Element(depth), pl.Element(lat_wide)), lambda i, s, c: (first + i, row, 0)),
            pl.BlockSpec((2, lanes), lambda i, s, c: (0, 0)),
        ]
        + [pl.BlockSpec((part, lanes), lambda i, s, c: (0, 0))] * chan_count
        + [HELD] * len(after),
        out_specs=pl.BlockSpec((bands, None, band_rows, lanes), lambda i, s, c: (0, i, 0, 0)),
        scratch_shapes=[pltpu.VMEM((plan["pad"] + plan["total"], lanes), BF16)],
    )
    return pl.pallas_call(
        functools.partial(synthesise_body, plan),
        grid_spec=spec,
        out_shape=jax.ShapeDtypeStruct((bands, count, band_rows, lanes), BF16),
        compiler_params=params(),
        cost_estimate=cost,
        name="synthesise",
    )(numbers, chan, table, parity_lanes(lanes), *parts, *after)


def split_groups(group_count, even):
    few = max(even, group_count // 6 // even * even)
    first = list(range(few))
    last = list(range(few, 2 * few))
    rest = list(range(2 * few, group_count))
    half = len(rest) // 2 // even * even
    return [first, rest[:half], rest[half:], last]


def on_device(signal, spectral_filter, channel_mix):
    lat_count = lax.axis_size("lat")
    chan_count = lax.axis_size("chan")
    lat_rows, quarter, lon_count = signal.shape
    lat_total = lat_rows * lat_count
    degrees = spectral_filter.shape[0]
    full_channels = channel_mix.shape[1]
    group_rows = 2 * lat_count
    group_count = degrees // group_rows
    lat_index = lax.axis_index("lat")
    chan_index = lax.axis_index("chan")
    chan = jnp.reshape(chan_index, (1,)).astype(jnp.int32)
    lanes = 4 * quarter

    kernels = lat_rows % BAND == 0 and quarter % BAND == 0 and (2 * lat_count) % BAND == 0 and group_count % 2 == 0
    pieces = split_groups(group_count, 2 if kernels else 1)

    e_at = jnp.arange(2, dtype=jnp.int32)
    group_orders = jnp.asarray(np.array([group_rows * g for p in pieces for g in p], np.int32))
    trig, synth = fourier_tables(group_orders, lat_count, lon_count)
    own_rows = lat_index * lat_rows + jnp.arange(lat_rows, dtype=jnp.int32)
    _, _, own_weight = latitude_terms(own_rows, lat_total, lon_count)
    cosine, log_sine, _ = latitude_terms(jnp.arange(lat_total, dtype=jnp.int32), lat_total, lon_count)
    orders_own = (group_orders[:, None] + 2 * lat_index + e_at[None, :]).reshape(-1)
    seeds = seed_logs(orders_own, log_sine)
    swap = swap_matrix()

    direct, cross = gain_tables(spectral_filter.reshape(degrees, 2 * full_channels), chan, quarter)

    last_moved = [None] * chan_count

    def moved(parts):
        out = [parts[0]]
        for shift in range(1, chan_count):
            pairs = [(i, (i + shift) % chan_count) for i in range(chan_count)]
            part = parts[shift]
            if last_moved[0] is not None:
                part = lax.optimization_barrier((part, last_moved[0]))[0]
            out.append(lax.ppermute(part, "chan", pairs))
        last_moved[0] = out[chan_count // 2]
        return out

    plans = [chunk_plan(groups, group_rows, degrees, chan_count) for groups in pieces]
    counts = [len(groups) for groups in pieces]
    edges = [sum(counts[:i]) for i in range(len(counts))]
    latest = [None]

    def queued(op, *args):
        held = tuple(x for x in latest if x is not None)
        del latest[1:]
        out = op(*args, after=held)
        latest[0] = out[0] if isinstance(out, (list, tuple)) else out
        return out

    chunks = len(plans)
    spectra, exchanged, tables, filtered, mixed, returned = {}, {}, {}, {}, {}, {}
    last_exchange = [None]

    def across_lat(x, *after):
        held = [a for a in after + (last_exchange[0],) if a is not None]
        if held:
            x = lax.optimization_barrier((x, *held))[0]
        last_exchange[0] = lax.all_to_all(x, "lat", split_axis=0, concat_axis=0, tiled=True)
        return last_exchange[0]

    def do_forward(which, cost):
        if kernels:
            first = edges[which[0]] * lat_count
            made = queued(
                forward_rows, signal, trig, own_weight, swap, first, [counts[i] for i in which],
                lat_count, cost
            )
            for i, out in zip(which, made):
                spectra[i] = out
            return
        for i in which:
            part = trig.reshape(4, group_count, lat_count, lon_count)[:, edges[i]:edges[i] + counts[i]]
            spectrum = jnp.einsum("jcn,qgkn->kgjqc", signal, part, preferred_element_type=F32)
            spectrum = (spectrum * own_weight[None, None, :, None, None]).astype(BF16)
            spectra[i] = spectrum.reshape(lat_count, counts[i], lat_rows, lanes)

    def do_exchange(i):
        exchanged[i] = across_lat(spectra[i])

    def do_table(which, cost):
        which = sorted(which, key=lambda i: pieces[i][0])
        joined = [g for i in which for g in pieces[i]]
        own_seeds = jnp.concatenate([seeds[2 * edges[i]:2 * (edges[i] + counts[i])] for i in which], 0)
        own_orders = jnp.concatenate([orders_own[2 * edges[i]:2 * (edges[i] + counts[i])] for i in which], 0)
        table = queued(
            legendre_table, joined, group_rows, own_seeds, own_orders.astype(F32), cosine, degrees, cost
        )
        for i in which:
            skip = pieces[i][0] - joined[0]
            tables[i] = (table, skip, skip * group_rows)

    def do_analyse(i, cost):
        filtered[i] = moved(
            queued(analyse, plans[i], chan, exchanged[i], tables[i], direct, cross, chan_count, cost)
        )

    def do_mix(i, cost):
        mixed[i] = moved(queued(mix, chan, filtered[i], kernel, cost))

    def do_synthesise(i, cost):
        back = queued(synthesise, plans[i], chan, tables[i], mixed[i], lat_count, cost)
        returned[i] = across_lat(back)

    do_forward([0, 1], LIGHT)
    do_exchange(0)
    do_table([0, 3], LIGHT)
    do_analyse(0, LIGHT)
    do_exchange(1)
    kernel = queued(mix_kernel, channel_mix, chan_count)
    do_forward([2, 3], LIGHT)
    do_mix(0, LIGHT)
    do_exchange(2)
    do_table([1, 2], HEAVY)
    do_analyse(1, LIGHT)
    do_exchange(3)
    do_synthesise(0, HEAVY)
    do_analyse(2, LIGHT)
    do_mix(1, HEAVY)
    do_analyse(3, LIGHT)
    do_synthesise(1, MEDIUM)
    do_mix(2, MEDIUM)
    do_mix(3, MEDIUM)
    do_synthesise(2, MEDIUM)
    do_synthesise(3, HEAVY)
    returned = [returned[i] for i in range(chunks)]
    if kernels:
        early = early_rows(returned[:-1], swap, lat_rows, quarter)
        return inverse_rows(early, returned[-1], synth, swap)
    rows = jnp.concatenate(returned, 1).reshape(lat_count, group_count, lat_rows, 4, quarter)
    synth = synth.reshape(4, group_count, lat_count, lon_count)
    output = jnp.einsum("kgjqd,qgkn->jdn", rows, synth, preferred_element_type=F32)
    return output.astype(BF16)


def solution(mesh):
    return jax.shard_map(
        on_device,
        mesh=mesh,
        in_specs=(P("lat", "chan", None), P(), P()),
        out_specs=P("lat", "chan", None),
        check_vma=False,
    )
```
